512 devices in a mesh: ctx: 16 (over z_hi, x), exp: 32 (over z_lo, y, core).
Axes of the slice: x: 4, y: 8, z: 8 (z_hi: 4, z_lo: 2; z = z_hi * 2 + z_lo), core: 2. Of those that a mesh axis runs over, the one named last changes fastest.
Arguments:
- hidden: bfloat16 [32, 128, 5120], P('exp', 'ctx'), may hold values from -6 to 6
- queries: bfloat16 [2048, 36864], P('ctx', 'exp'), may hold values from -50 to 50
- latents: bfloat16 [2048, 576], P('ctx'), may hold values from -6.5 to 6.5
- expert_ids: int32 [32, 128, 6], P('exp', 'ctx'), may hold values from 0 to 31, all different within a row; in each aligned block of 8 rows (0 to 7, 8 to 15, ..., all dimensions but the last counted through in order) at most 2 rows name the same one
- route_weight: float32 [32, 128, 6], P('exp', 'ctx'), may hold values from 0.1 to 1
- w_gate: bfloat16 [32, 1536, 5120], P('exp', 'ctx'), may hold values from -0.078125 to 0.078125
- w_up: bfloat16 [32, 1536, 5120], P('exp', 'ctx'), may hold values from -0.078125 to 0.078125
- w_down: bfloat16 [32, 5120, 1536], P('exp', 'ctx'), may hold values from -0.15625 to 0.15625
Outputs:
- attended: bfloat16 [2048, 32768], P('ctx', 'exp')
- moe_out: bfloat16 [32, 128, 5120], P('exp', 'ctx')
The draws below stay inside these ranges and needn't reach their ends.
Inputs may be any that keep to these rules, and one draw needn't show every extreme that they name: `expert_ids`: each token names 6 different experts. Within the 8 rows of one device (aligned blocks of rows of one group) no expert is named by more than 2 rows, a bound that some block reaches.
All inputs are finite; a program needn't handle non-finite values.
Results may differ from the reference program's by a relative error of at most 0.0057.
Values may be sent and summed in bfloat16 or wider, within the bound.
A program may use at most 64 MiB of HBM per device.

```python
import math
import jax
import jax.numpy as jnp
import numpy as np
from jax import lax

D = 5120
LATENT = 512
ROPE = 64
HID = 1536
TOPK = 6
HEADS = 64
TOK_DEV = 128
MOE_DEV = 8
EXPERTS = 32
CAP = 2
MAXROWS = 1024
GROUPS = 32
ROWS = 128
LEN = 2048
N_EXP = 32


def latent_pair(key):
    base = jax.random.fold_in(key, 4711)
    key_kv, key_q = jax.random.split(base, 2)
    width = LATENT + ROPE
    latent = jnp.clip(jax.random.normal(key_kv, (LEN, width), jnp.float32), -6.0, 6.0)
    query = jnp.clip(jax.random.normal(key_q, (LEN, HEADS, width), jnp.float32), -6.0, 6.0)
    return (query.reshape(LEN, HEADS * width), latent)


def draw_queries(key, part):
    return latent_pair(key)[0].astype(jnp.bfloat16)


def draw_latents(key, part):
    return latent_pair(key)[1].astype(jnp.bfloat16)


def levels(key, shape, shards, smallest, top_value):
    gain = 1.0
    for position, shards_of in shards:
        steps = jax.random.uniform(jax.random.fold_in(jax.random.fold_in(key, 6), position), (shards_of,), jnp.float32, smallest / len(shards), top_value / len(shards))
        gain = gain * jnp.repeat(jnp.exp(steps), shape[position] // shards_of).reshape((-1,) + (1,) * (len(shape) - 1 - position))
    return gain


def assign_block(stream_key, own, number, rows, number_of, top, limit, skew):
    order = jax.random.permutation(stream_key, number_of)
    packed, ordinary = shares(number_of, rows * top, limit, skew, True), shares(number_of, rows * top, limit, skew, False)
    places = jnp.arange(number_of)

    def named(sizes, offset_by):
        used = int((sizes > 0).sum())
        fixed = max(1, used // 4)
        shifted = fixed + (places - fixed + offset_by * (used - fixed)) % max(1, number_of - fixed)
        return jnp.zeros((number_of,), jnp.int32).at[order[jnp.where(places < fixed, places, shifted)]].set(jnp.asarray(sizes, jnp.int32))

    sizes = jnp.where(number % 4 == 0, named(packed, number // 4), named(ordinary, number - number // 4 - 1))
    mixed = jax.random.permutation(jax.random.fold_in(own, 3), number_of)
    source_of, receiver = mixed[0:number_of // 2 * 2:2], mixed[1:number_of // 2 * 2:2]
    slack = jnp.minimum(sizes[source_of] - 1, limit - sizes[receiver]) // 2
    slack = jnp.where((source_of == order[0]) | (receiver == order[0]) | (sizes[receiver] == 0), 0, jnp.maximum(slack, 0))
    shifted = jax.random.randint(jax.random.fold_in(own, 4), (number_of // 2,), 0, 1 << 20) % (slack + 1)
    sizes = sizes.at[source_of].add(-shifted).at[receiver].add(shifted)
    labels = jnp.searchsorted(jnp.cumsum(sizes), jnp.arange(rows * top), side="right").astype(jnp.int32)
    grid = labels.reshape(top, rows).T
    grid = grid[jax.random.permutation(jax.random.fold_in(own, 1), rows)]
    offset_by = jax.random.randint(jax.random.fold_in(own, 2), (rows, 1), 0, top)
    return jnp.take_along_axis(grid, (jnp.arange(top)[None, :] + offset_by) % top, axis=1)


def shares(number_of, total, bound, lean, full):
    portions = [(1 << 20) // math.isqrt(grade ** lean) + 1 for grade in range(1, number_of + 1)]
    largest = bound if full else min(bound, max(-(-total // number_of), total * portions[0] // sum(portions)))
    least = 1 if total - largest >= number_of - 1 else 0
    counts, spare = [largest] + [least] * (number_of - 1), total - largest - least * (number_of - 1)
    while spare > 0:
        candidates = [i for i in range(1, number_of) if counts[i] < largest] or [i for i in range(1, number_of) if counts[i] < bound]
        pool, budget = sum([portions[i] for i in candidates]), spare
        for i in candidates:
            extra = min(bound - counts[i], max(1, budget * portions[i] // pool), spare)
            counts[i] = counts[i] + extra
            spare = spare - extra
    return np.array(counts)


def normal_values(stream_key, shape, scale, reach, cuts=(), kind=jnp.bfloat16):
    entries = scale * jax.random.normal(stream_key, shape, jnp.float32)
    if cuts:
        entries = entries * levels(stream_key, shape, cuts, -0.22, 0.18)
    return jnp.clip(entries, -reach, reach).astype(kind)


def setup_inputs(seed: int = 0) -> dict:
    streams_of = jax.random.split(jax.random.key(seed), 9)
    hidden = normal_values(streams_of[0], (GROUPS, ROWS, D), 1.0, 6.0, ((0, 32), (1, 16)))
    queries = draw_queries(jax.random.fold_in(streams_of[8], 71), 0)
    latents = draw_latents(jax.random.fold_in(streams_of[8], 71), 0)
    expert_ids_keys = jax.random.split(jax.random.fold_in(streams_of[3], 1), GROUPS * ROWS // MOE_DEV)
    expert_ids_turns = jax.random.permutation(jax.random.fold_in(streams_of[3], 3), GROUPS * ROWS // MOE_DEV)
    expert_ids = jax.vmap(lambda own, number: assign_block(jax.random.fold_in(streams_of[3], 2), own, number, MOE_DEV, N_EXP, TOPK, CAP, 0))(expert_ids_keys, expert_ids_turns).reshape((GROUPS, ROWS, TOPK))
    route_weight = jnp.clip(0.1 + 0.9 * jax.random.uniform(streams_of[4], (GROUPS, ROWS, TOPK), jnp.float32) ** levels(streams_of[4], (GROUPS, ROWS, TOPK), ((0, 32), (1, 16)), -0.2, 0.2), 0.1, 1.0)
    w_gate = normal_values(streams_of[5], (EXPERTS, HID, D), D ** -0.5, 0.078125, ((0, 32), (1, 16)))
    w_up = normal_values(streams_of[6], (EXPERTS, HID, D), D ** -0.5, 0.078125, ((0, 32), (1, 16)))
    w_down = normal_values(streams_of[7], (EXPERTS, D, HID), HID ** -0.5, 0.15625, ((0, 32), (1, 16)))
    return {"hidden": hidden, "queries": queries, "latents": latents, "expert_ids": expert_ids, "route_weight": route_weight, "w_gate": w_gate, "w_up": w_up, "w_down": w_down}


SCALE = 0.07216878364870322


def attend(queries, latents):
    length = latents.shape[0]
    width = LATENT + ROPE
    qv = queries.reshape(length, HEADS, width)
    keys = latents.astype(jnp.float32)
    pos = jnp.arange(length, dtype=jnp.int32)
    block = pos // TOK_DEV
    same = (block[:, None] == block[None, :]) & (pos[None, :] <= pos[:, None])
    before = block[None, :] == block[:, None] - 1
    visible = same | before

    def one_head(index):
        query_head = lax.dynamic_index_in_dim(qv, index, 1, keepdims=False).astype(jnp.float32)
        scores = jnp.einsum("ic,jc->ij", query_head, keys) * SCALE
        scores = jnp.where(visible, scores, jnp.float32(-1e30))
        top = jnp.max(scores, axis=-1, keepdims=True)
        expo = jnp.exp(scores - top)
        probs = (expo / jnp.sum(expo, axis=-1, keepdims=True)).astype(jnp.bfloat16)
        result = jnp.einsum("ij,jc->ic", probs.astype(jnp.float32), keys[:, :LATENT])
        return result.astype(jnp.bfloat16)

    per_head = lax.map(one_head, jnp.arange(HEADS, dtype=jnp.int32))
    return jnp.transpose(per_head, (1, 0, 2)).reshape(length, HEADS * LATENT)


def reference(hidden, queries, latents, expert_ids, route_weight, w_gate, w_up, w_down):
    attended = attend(queries, latents)
    rows_all = hidden.reshape(-1, D)
    picks = expert_ids.reshape(-1, TOPK)
    weights = route_weight.reshape(-1, TOPK)

    def one_expert(total, index):
        hit = picks == index
        rowhit = jnp.any(hit, axis=1)
        count = jnp.sum(rowhit.astype(jnp.int32))
        chosen = jnp.nonzero(rowhit, size=MAXROWS, fill_value=0)[0].astype(jnp.int32)
        valid = jnp.arange(MAXROWS, dtype=jnp.int32) < count
        coef = jnp.sum(jnp.where(hit, weights, jnp.zeros_like(weights)), axis=1)[chosen]
        coef = jnp.where(valid, coef, jnp.zeros_like(coef))
        rows = rows_all[chosen]
        gate_w = lax.dynamic_index_in_dim(w_gate, index, 0, keepdims=False)
        up_w = lax.dynamic_index_in_dim(w_up, index, 0, keepdims=False)
        down_w = lax.dynamic_index_in_dim(w_down, index, 0, keepdims=False)
        gate = jnp.dot(rows, gate_w.T, preferred_element_type=jnp.float32)
        upper = jnp.dot(rows, up_w.T, preferred_element_type=jnp.float32)
        act = (jax.nn.silu(gate) * upper).astype(jnp.bfloat16)
        out_rows = jnp.dot(act, down_w.T, preferred_element_type=jnp.float32).astype(jnp.bfloat16)
        total = total.at[chosen].add(coef[:, None] * out_rows.astype(jnp.float32))
        return total, None

    start = jnp.zeros((rows_all.shape[0], D), jnp.float32)
    total, _ = lax.scan(one_expert, start, jnp.arange(EXPERTS, dtype=jnp.int32))
    moe_out = total.astype(jnp.bfloat16).reshape(hidden.shape)
    return attended, moe_out
```

```python
import functools

import jax
import jax.numpy as jnp
from jax import lax
from jax.experimental import pallas as pl
from jax.experimental.pallas import tpu as pltpu
from jax.sharding import PartitionSpec as P

LATENT = 512
ROPE = 64
SCALE = 0.07216878364870322
NX = 4
NZ = 4
CAP = 2
MESH = pl.DeviceIdType.MESH
F32, BF16 = jnp.float32, jnp.bfloat16


def shifted(block, axis, distance):
    devices = range(lax.axis_size(axis))
    route = [(i - distance, i) for i in devices if i - distance in devices]
    return lax.ppermute(block, axis, route)


def dot_nt(left, right):
    return lax.dot_general(left, right, (((1,), (1,)), ((), ())), preferred_element_type=F32)


def flat(ref):
    blocks, inner, width = ref.shape
    return ref[...].reshape(blocks * inner, width)


def moe_kernel(
    n_exp,
    tok_ref, pick_ref, weight_ref, wg_ref, wu_ref, wd_ref, out_ref,
    tokens, table, own_table, packed, rows, gate_w, up_w, down_w, act, y_send, y_recv, mixed, final,
    local_sem, tok_s, tok_r, table_s, table_r, row_s, row_r, w_s, w_r, act_s, act_r, y_s, y_r, fin_s, fin_r,
):
    c, e = lax.axis_index("ctx"), lax.axis_index("exp")
    z, x = c // NX, c % NX
    tok, width = tok_ref.shape[1], tok_ref.shape[2]
    units, cols = wg_ref.shape[1], wd_ref.shape[1]
    chunk = NZ * CAP
    slots = n_exp * chunk
    out_cols = NX * cols
    right = (z * NX + (x + 1) % NX, e)
    left = (z * NX + (x + NX - 1) % NX, e)
    x_left, x_right = (x + NX - 1) % NX, (x + 1) % NX

    def z_peer(d):
        return ((z + d) % NZ) * NX + x

    def at(ref, index, size):
        return ref.at[pl.ds(pl.multiple_of(index * size, size), size), :]

    own = [
        pltpu.make_async_copy(src.at[0], at(dst, x, size), local_sem.at[i])
        for i, (src, dst, size) in enumerate(
            ((wg_ref, gate_w, units), (wu_ref, up_w, units), (wd_ref, down_w, cols))
        )
    ]
    for copy in own:
        copy.start()

    barrier = pltpu.get_barrier_semaphore()

    def greet(d, carry):
        pl.semaphore_signal(barrier, inc=1, device_id=(c, lax.rem(e + d, n_exp)), device_id_type=MESH)
        return carry

    lax.fori_loop(1, n_exp, greet, 0)
    for d in range(1, NZ):
        pl.semaphore_signal(barrier, inc=1, device_id=(z_peer(d), e), device_id_type=MESH)
    for peer in (left, right):
        pl.semaphore_signal(barrier, inc=1, device_id=peer, device_id_type=MESH)

    lane = lax.broadcasted_iota(jnp.int32, (tok, slots), 1)
    lane_expert, lane_z, lane_rank = lane // chunk, (lane % chunk) // CAP, lane % CAP
    picks, weights = pick_ref[0], weight_ref[0]
    named = jnp.zeros((tok, slots), F32)
    coef = jnp.zeros((tok, slots), F32)
    for k in range(picks.shape[1]):
        hit = picks[:, k : k + 1] == lane_expert
        named = jnp.where(hit, 1.0, named)
        coef = jnp.where(hit, weights[:, k : k + 1], coef)
    before = lax.broadcasted_iota(jnp.int32, (tok, tok), 1) < lax.broadcasted_iota(jnp.int32, (tok, tok), 0)
    rank = jnp.dot(jnp.where(before, 1.0, 0.0), named, preferred_element_type=F32)
    here = (lane_z == z) & (rank == lane_rank.astype(F32))
    own_table[0:tok, :] = jnp.where(here, coef, 0.0)
    own_table[tok : 2 * tok, :] = jnp.where(here, named, 0.0)

    pl.semaphore_wait(barrier, n_exp - 1 + NZ - 1 + 2)

    def remote(src, dst, send, recv, peer):
        return pltpu.make_async_remote_copy(
            src_ref=src, dst_ref=dst, send_sem=send, recv_sem=recv, device_id=peer, device_id_type=MESH
        )

    for d in range(1, NZ):
        remote(own_table, table.at[z], table_s.at[d], table_r.at[z], (z_peer(d), e)).start()
        remote(tok_ref.at[0], tokens.at[z], tok_s.at[d], tok_r.at[z], (z_peer(d), e)).start()
    tokens[z] = tok_ref[0]
    table[z] = own_table[...]

    own[0].wait()
    own[1].wait()
    mine_g, mine_u = at(gate_w, x, units), at(up_w, x, units)
    to_right = [
        remote(mine_g, mine_g, w_s.at[0], w_r.at[0], right),
        remote(mine_u, mine_u, w_s.at[1], w_r.at[1], right),
    ]
    to_left = [
        remote(mine_u, mine_u, w_s.at[2], w_r.at[2], left),
        remote(mine_g, mine_g, w_s.at[3], w_r.at[3], left),
    ]
    for a, b in zip(to_right, to_left):
        a.start()
        b.start()

    for d in range(1, NZ):
        p = (z + d) % NZ
        remote(own_table, table.at[p], table_s.at[d], table_r.at[p], (c, e)).wait_recv()
        remote(tok_ref.at[0], tokens.at[p], tok_s.at[d], tok_r.at[p], (c, e)).wait_recv()

    select = jnp.concatenate([table[i, tok : 2 * tok, :] for i in range(NZ)], axis=0)
    select = jnp.transpose(select, (1, 0)).astype(BF16)
    picked = jnp.dot(select, flat(tokens), preferred_element_type=F32)
    packed[...] = picked.reshape(packed.shape).astype(BF16)

    def row_copy(peer, src_index, dst_index, s, r):
        return remote(packed.at[src_index], rows.at[dst_index], row_s.at[s], row_r.at[r], (c, peer))

    def send_rows(d, carry):
        peer = lax.rem(e + d, n_exp)
        row_copy(peer, peer, e, peer, e).start()
        return carry

    lax.fori_loop(1, n_exp, send_rows, 0)
    rows[e] = packed[e]

    theirs_g, theirs_u = at(gate_w, x_left, units), at(up_w, x_right, units)
    remote(theirs_g, theirs_g, w_s.at[0], w_r.at[0], right).wait_recv()
    on_right = remote(theirs_g, theirs_g, w_s.at[4], w_r.at[4], right)
    on_right.start()
    remote(theirs_u, theirs_u, w_s.at[2], w_r.at[2], left).wait_recv()
    on_left = remote(theirs_u, theirs_u, w_s.at[5], w_r.at[5], left)
    on_left.start()
    to_right[0].wait_send()
    to_right[1].wait_send()
    to_left[0].wait_send()
    to_left[1].wait_send()
    up_left, gate_right = at(up_w, x_left, units), at(gate_w, x_right, units)
    remote(up_left, up_left, w_s.at[1], w_r.at[1], right).wait_recv()
    remote(gate_right, gate_right, w_s.at[3], w_r.at[3], left).wait_recv()
    on_right.wait_send()
    on_left.wait_send()
    far = (x + 2) % NX
    far_g, far_u = at(gate_w, far, units), at(up_w, far, units)

    own[2].wait()
    mine_d = at(down_w, x, cols)
    d_right = remote(mine_d, mine_d, w_s.at[6], w_r.at[6], right)
    d_left = remote(mine_d, mine_d, w_s.at[7], w_r.at[7], left)
    d_right.start()
    d_left.start()

    remote(far_g, far_g, w_s.at[4], w_r.at[4], right).wait_recv()
    remote(far_u, far_u, w_s.at[5], w_r.at[5], left).wait_recv()

    def take_rows(d, carry):
        peer = lax.rem(e + d, n_exp)
        row_copy(e, peer, peer, peer, peer).wait_recv()
        return carry

    lax.fori_loop(1, n_exp, take_rows, 0)

    chosen = flat(rows)
    gate = dot_nt(chosen, gate_w[...])
    upper = dot_nt(chosen, up_w[...])
    act[z] = (gate / (1.0 + jnp.exp(-gate)) * upper).astype(BF16)
    for d in range(1, NZ):
        remote(act.at[z], act.at[z], act_s.at[d], act_r.at[z], (z_peer(d), e)).start()

    half = cols // 2

    def half_of(index, part):
        return down_w.at[pl.ds(pl.multiple_of(index * cols + part * half, half), half), :]

    left_d, right_d = at(down_w, x_left, cols), at(down_w, x_right, cols)
    remote(left_d, left_d, w_s.at[6], w_r.at[6], right).wait_recv()
    f_right = remote(half_of(x_left, 0), half_of(x_left, 0), w_s.at[8], w_r.at[8], right)
    f_right.start()
    remote(right_d, right_d, w_s.at[7], w_r.at[7], left).wait_recv()
    f_left = remote(half_of(x_right, 1), half_of(x_right, 1), w_s.at[9], w_r.at[9], left)
    f_left.start()
    for d in range(1, NZ):
        p = (z + d) % NZ
        remote(act.at[p], act.at[p], act_s.at[d], act_r.at[p], (c, e)).wait_recv()
    remote(half_of(far, 0), half_of(far, 0), w_s.at[8], w_r.at[8], right).wait_recv()
    remote(half_of(far, 1), half_of(far, 1), w_s.at[9], w_r.at[9], left).wait_recv()

    y = jnp.zeros((slots, out_cols), F32)
    per_z = NX * units
    for i in range(NZ):
        y = y + dot_nt(act[i], down_w[:, i * per_z : (i + 1) * per_z])
    y_send[...] = y.reshape(y_send.shape).astype(BF16)

    def y_copy(peer, src_index, dst_index, s, r):
        return remote(y_send.at[src_index], y_recv.at[dst_index], y_s.at[s], y_r.at[r], (c, peer))

    def send_y(d, carry):
        peer = lax.rem(e + d, n_exp)
        y_copy(peer, peer, e, peer, e).start()
        return carry

    lax.fori_loop(1, n_exp, send_y, 0)
    y_recv[e] = y_send[e]

    def take_y(d, carry):
        peer = lax.rem(e + d, n_exp)
        y_copy(e, peer, peer, peer, peer).wait_recv()
        return carry

    lax.fori_loop(1, n_exp, take_y, 0)

    combine = jnp.concatenate([table[i, 0:tok, :] for i in range(NZ)], axis=0)
    high = combine.astype(BF16)
    low = (combine - high.astype(F32)).astype(BF16)
    arrived = flat(y_recv)
    total = jnp.dot(high, arrived, preferred_element_type=F32)
    total = total + jnp.dot(low, arrived, preferred_element_type=F32)
    mixed[...] = total.reshape(mixed.shape).astype(BF16)

    def columns(index):
        return final.at[:, pl.ds(pl.multiple_of(index * out_cols, out_cols), out_cols)]

    for d in range(1, NZ):
        p = (z + d) % NZ
        remote(mixed.at[p], columns(z), fin_s.at[d], fin_r.at[z], (z_peer(d), e)).start()
    columns(z)[...] = mixed[z]
    for d in range(1, NZ):
        p = (z + d) % NZ
        remote(mixed.at[p], columns(p), fin_s.at[d], fin_r.at[p], (c, e)).wait_recv()
    out_ref[0] = final[...]

    for d in range(1, NZ):
        p = (z + d) % NZ
        remote(own_table, table.at[z], table_s.at[d], table_r.at[z], (z_peer(d), e)).wait_send()
        remote(tok_ref.at[0], tokens.at[z], tok_s.at[d], tok_r.at[z], (z_peer(d), e)).wait_send()
        remote(act.at[z], act.at[z], act_s.at[d], act_r.at[z], (z_peer(d), e)).wait_send()
        remote(mixed.at[p], columns(z), fin_s.at[d], fin_r.at[z], (z_peer(d), e)).wait_send()
    for copy in (d_right, d_left, f_right, f_left):
        copy.wait_send()

    def sent(d, carry):
        peer = lax.rem(e + d, n_exp)
        row_copy(peer, peer, e, peer, e).wait_send()
        y_copy(peer, peer, e, peer, e).wait_send()
        return carry

    lax.fori_loop(1, n_exp, sent, 0)


def routed(hidden, expert_ids, route_weight, w_gate, w_up, w_down):
    n_exp = lax.axis_size("exp")
    tok, width = hidden.shape[1:]
    units, hid = w_gate.shape[1], w_down.shape[2]
    cols = w_down.shape[1]
    slots = n_exp * NZ * CAP
    dma = pltpu.SemaphoreType.DMA
    vmem = pl.BlockSpec(memory_space=pltpu.VMEM)
    hbm = pl.BlockSpec(memory_space=pl.ANY)
    return pl.pallas_call(
        functools.partial(moe_kernel, n_exp),
        out_shape=jax.ShapeDtypeStruct(hidden.shape, BF16),
        in_specs=[vmem, vmem, vmem, hbm, hbm, hbm],
        out_specs=vmem,
        scratch_shapes=[
            pltpu.VMEM((NZ, tok, width), BF16),
            pltpu.VMEM((NZ, 2 * tok, slots), F32),
            pltpu.VMEM((2 * tok, slots), F32),
            pltpu.VMEM((n_exp, NZ * CAP, width), BF16),
            pltpu.VMEM((n_exp, NZ * CAP, width), BF16),
            pltpu.VMEM((NX * units, width), BF16),
            pltpu.VMEM((NX * units, width), BF16),
            pltpu.VMEM((NX * cols, hid), BF16),
            pltpu.VMEM((NZ, slots, NX * units), BF16),
            pltpu.VMEM((n_exp, NZ * CAP, NX * cols), BF16),
            pltpu.VMEM((n_exp, NZ * CAP, NX * cols), BF16),
            pltpu.VMEM((NZ, tok, NX * cols), BF16),
            pltpu.VMEM((tok, width), BF16),
            dma((3,)),
            dma((NZ,)), dma((NZ,)), dma((NZ,)), dma((NZ,)),
            dma((n_exp,)), dma((n_exp,)),
            dma((10,)), dma((10,)),
            dma((NZ,)), dma((NZ,)),
            dma((n_exp,)), dma((n_exp,)),
            dma((NZ,)), dma((NZ,)),
        ],
        compiler_params=pltpu.CompilerParams(
            collective_id=0, has_side_effects=True, vmem_limit_bytes=50 << 20
        ),
    )(hidden, expert_ids, route_weight, w_gate, w_up, w_down)


def on_device(hidden, queries, latents, expert_ids, route_weight, w_gate, w_up, w_down):
    tok_att = latents.shape[0]
    heads_dev = queries.shape[1] // (LATENT + ROPE)
    earlier_kv = shifted(latents, "ctx", 1)
    keys = jnp.concatenate([earlier_kv, latents], axis=0)
    query_rows = queries.reshape(tok_att, heads_dev, LATENT + ROPE)
    scores = jnp.einsum("thc,kc->htk", query_rows, keys, preferred_element_type=F32) * SCALE
    row_pos = jnp.arange(tok_att, dtype=jnp.int32)
    key_pos = jnp.arange(2 * tok_att, dtype=jnp.int32)
    seen_own = (key_pos[None, :] >= tok_att) & (key_pos[None, :] - tok_att <= row_pos[:, None])
    seen_prev = (key_pos[None, :] < tok_att) & (lax.axis_index("ctx") > 0)
    scores = jnp.where((seen_own | seen_prev)[None, :, :], scores, jnp.float32(-1e30))
    top = jnp.max(scores, axis=-1, keepdims=True)
    expo = jnp.exp(scores - top)
    probs = (expo / jnp.sum(expo, axis=-1, keepdims=True)).astype(BF16)
    mixed_heads = jnp.einsum("htk,kc->thc", probs, keys[:, :LATENT], preferred_element_type=F32)
    attended = mixed_heads.astype(BF16).reshape(tok_att, heads_dev * LATENT)
    moe_out = routed(hidden, expert_ids, route_weight, w_gate, w_up, w_down)
    return attended, moe_out


def solution(mesh):
    placed = (
        P("exp", "ctx", None),
        P("ctx", "exp"),
        P("ctx", None),
        P("exp", "ctx", None),
        P("exp", "ctx", None),
        P("exp", "ctx", None),
        P("exp", "ctx", None),
        P("exp", "ctx", None),
    )
    return jax.shard_map(
        on_device,
        mesh=mesh,
        in_specs=placed,
        out_specs=(P("ctx", "exp"), P("exp", "ctx", None)),
        check_vma=False,
    )
```

```python
import functools

import jax
import jax.numpy as jnp
from jax import lax
from jax.experimental import pallas as pl
from jax.experimental.pallas import tpu as pltpu
from jax.sharding import PartitionSpec as P

LATENT = 512
ROPE = 64
SCALE = 0.07216878364870322
NX = 4
NZ = 4
CAP = 2
MESH = pl.DeviceIdType.MESH
F32, BF16 = jnp.float32, jnp.bfloat16


def dot_nt(left, right):
    return lax.dot_general(left, right, (((1,), (1,)), ((), ())), preferred_element_type=F32)


def flat(ref):
    value = ref[...]
    return value.reshape(-1, value.shape[-1])


def moe_kernel(
    n_exp,
    tok_ref, pick_ref, weight_ref, q_ref, lat_ref, wg_ref, wu_ref, wd_ref, out_ref, att_ref,
    prev, tokens, table, own_table, thin_send, thin, wide_send, wide, chosen, gate_up, down_w, act,
    y_send, y_recv, mixed, final,
    local_sem, lat_s, lat_r, tok_s, tok_r, table_s, table_r, thin_s, thin_r, spread_s, spread_r, wide_s, wide_r,
    w_s, w_r, act_s, act_r, y_s, y_r, fin_s, fin_r,
):
    c, e = lax.axis_index("ctx"), lax.axis_index("exp")
    n_ctx = NX * NZ
    z, x = c // NX, c % NX
    tok, width = tok_ref.shape[1], tok_ref.shape[2]
    units, cols = wg_ref.shape[1], wd_ref.shape[1]
    chunk = NZ * CAP
    slots = n_exp * chunk
    half = width // 2
    part = half // NZ
    x_left, x_right, far = (x + NX - 1) % NX, (x + 1) % NX, (x + 2) % NX
    right, left = (z * NX + x_right, e), (z * NX + x_left, e)
    after, before = (lax.rem(c + 1, n_ctx), e), (lax.rem(c + n_ctx - 1, n_ctx), e)
    me = (c, e)

    def z_peer(d):
        return ((z + d) % NZ) * NX + x

    def at(ref, start, size, step):
        return ref.at[pl.ds(pl.multiple_of(start, step), size), :]

    def gate_of(index):
        return at(gate_up, index * 2 * units, units, units)

    def up_of(index):
        return at(gate_up, index * 2 * units + units, units, units)

    def down_of(index):
        return at(down_w, index * cols, cols, cols)

    def down_part(index, k):
        return at(down_w, index * cols + k * (cols // 2), cols // 2, cols // 2)

    def remote(src, dst, send, recv, peer):
        return pltpu.make_async_remote_copy(
            src_ref=src, dst_ref=dst, send_sem=send, recv_sem=recv, device_id=peer, device_id_type=MESH
        )

    own = [
        pltpu.make_async_copy(src.at[0], dst, local_sem.at[i])
        for i, (src, dst) in enumerate(((wg_ref, gate_of(x)), (wu_ref, up_of(x)), (wd_ref, down_of(x))))
    ]
    for copy in own:
        copy.start()

    barrier = pltpu.get_barrier_semaphore()
    for peer in [left, right, before, after] + [(z_peer(d), e) for d in range(1, NZ)]:
        pl.semaphore_signal(barrier, inc=1, device_id=peer, device_id_type=MESH)

    def greet(d, carry):
        pl.semaphore_signal(barrier, inc=1, device_id=(c, lax.rem(e + d, n_exp)), device_id_type=MESH)
        return carry

    lax.fori_loop(1, n_exp, greet, 0)

    lane = lax.broadcasted_iota(jnp.int32, (tok, slots), 1)
    lane_expert, inner = lane // chunk, lane % chunk
    picks, weights = pick_ref[0], weight_ref[0]
    named = jnp.zeros((tok, slots), F32)
    coef = jnp.zeros((tok, slots), F32)
    for k in range(picks.shape[1]):
        hit = picks[:, k : k + 1] == lane_expert
        named = jnp.where(hit, 1.0, named)
        coef = jnp.where(hit, weights[:, k : k + 1], coef)
    lower = lax.broadcasted_iota(jnp.int32, (tok, tok), 1) < lax.broadcasted_iota(jnp.int32, (tok, tok), 0)
    rank = jnp.dot(jnp.where(lower, 1.0, 0.0), named, preferred_element_type=F32)
    here = (inner // CAP == z) & (rank == (inner % CAP).astype(F32))
    own_table[0:tok, :] = jnp.where(here, coef, 0.0)
    own_table[tok : 2 * tok, :] = jnp.where(here, named, 0.0)
    taken = jnp.where(rank == (inner // NZ).astype(F32), named, 0.0)
    thin_pick = jnp.concatenate([jnp.where(inner % NZ == k, taken, 0.0) for k in range(NZ)], axis=0)
    thin_pick = jnp.transpose(thin_pick, (1, 0)).astype(BF16)
    first = tok_ref[0, :, 0:half].astype(F32)
    first = jnp.concatenate([first[:, k * part : (k + 1) * part] for k in range(NZ)], axis=0).astype(BF16)
    thin_send[...] = jnp.dot(thin_pick, first, preferred_element_type=F32).reshape(thin_send.shape).astype(BF16)

    own[0].wait()
    own[1].wait()
    pl.semaphore_wait(barrier, n_exp - 1 + NZ - 1 + 4)

    g_right = remote(gate_of(x), gate_of(x), w_s.at[0], w_r.at[0], right)
    u_right = remote(up_of(x), up_of(x), w_s.at[1], w_r.at[1], right)
    u_left = remote(up_of(x), up_of(x), w_s.at[2], w_r.at[2], left)
    g_left = remote(gate_of(x), gate_of(x), w_s.at[3], w_r.at[3], left)
    for copy in (g_right, u_left, u_right, g_left):
        copy.start()

    second = tok_ref.at[0, :, pl.ds(half, half)]
    for d in range(1, NZ):
        remote(own_table, table.at[z], table_s.at[d], table_r.at[z], (z_peer(d), e)).start()
        remote(second, tokens.at[z], tok_s.at[d], tok_r.at[z], (z_peer(d), e)).start()
    tokens[z] = tok_ref[0, :, half:width]
    table[z] = own_table[...]

    def thin_copy(peer):
        return remote(thin_send.at[peer], thin.at[e, z], thin_s, thin_r, (c, peer))

    def send_thin(d, carry):
        thin_copy(lax.rem(e + d, n_exp)).start()
        return carry

    pltpu.make_async_copy(thin_send.at[e], thin.at[e, z], thin_r).start()
    lax.fori_loop(1, n_exp, send_thin, 0)
    lat_copy = remote(lat_ref, prev, lat_s, lat_r, after)
    lat_copy.start()

    for d in range(1, NZ):
        p = (z + d) % NZ
        remote(own_table, table.at[p], table_s.at[d], table_r.at[p], me).wait_recv()
        remote(second, tokens.at[p], tok_s.at[d], tok_r.at[p], me).wait_recv()

    select = jnp.concatenate([table[i, tok : 2 * tok, :] for i in range(NZ)], axis=0)
    select = jnp.transpose(select, (1, 0)).astype(BF16)
    wide_send[...] = jnp.dot(select, flat(tokens), preferred_element_type=F32).reshape(wide_send.shape).astype(BF16)

    def send_wide(d, carry):
        peer = lax.rem(e + d, n_exp)
        remote(wide_send.at[peer], wide.at[e], wide_s, wide_r, (c, peer)).start()
        return carry

    pltpu.make_async_copy(wide_send.at[e], wide.at[e], wide_r).start()
    lax.fori_loop(1, n_exp, send_wide, 0)

    column = thin.at[:, z]
    remote(column, column, thin_s, thin_r, me).wait_recv()
    for d in range(1, NZ):
        remote(column, column, spread_s.at[d], spread_r.at[z], (z_peer(d), e)).start()

    lat_copy.wait_recv()
    n_att = lat_ref.shape[0]
    row = lax.broadcasted_iota(jnp.int32, (n_att, n_att), 0)
    col = lax.broadcasted_iota(jnp.int32, (n_att, n_att), 1)
    low = jnp.float32(-1e30)
    depth = LATENT + ROPE
    for h in range(q_ref.shape[1] // depth):
        query = q_ref[:, h * depth : (h + 1) * depth]
        s_own = jnp.where(col <= row, dot_nt(query, lat_ref[...]) * SCALE, low)
        s_prev = jnp.where(c > 0, dot_nt(query, prev[...]) * SCALE, low)
        top = jnp.maximum(jnp.max(s_own, axis=1, keepdims=True), jnp.max(s_prev, axis=1, keepdims=True))
        e_own, e_prev = jnp.exp(s_own - top), jnp.exp(s_prev - top)
        total = jnp.sum(e_own, axis=1, keepdims=True) + jnp.sum(e_prev, axis=1, keepdims=True)
        value = jnp.dot((e_own / total).astype(BF16), lat_ref[:, 0:LATENT], preferred_element_type=F32)
        value = value + jnp.dot((e_prev / total).astype(BF16), prev[:, 0:LATENT], preferred_element_type=F32)
        att_ref[:, h * LATENT : (h + 1) * LATENT] = value.astype(BF16)

    remote(gate_of(x_left), gate_of(x_left), w_s.at[0], w_r.at[0], me).wait_recv()
    g_on = remote(gate_of(x_left), gate_of(x_left), w_s.at[4], w_r.at[4], right)
    g_on.start()
    remote(up_of(x_right), up_of(x_right), w_s.at[2], w_r.at[2], me).wait_recv()
    u_on = remote(up_of(x_right), up_of(x_right), w_s.at[5], w_r.at[5], left)
    u_on.start()

    for d in range(1, NZ):
        p = (z + d) % NZ
        remote(thin.at[:, p], thin.at[:, p], spread_s.at[d], spread_r.at[p], me).wait_recv()
    block = NZ * chunk * NZ
    r_out = lax.broadcasted_iota(jnp.int32, (block, block), 0)
    r_in = lax.broadcasted_iota(jnp.int32, (block, block), 1)
    per = block // NZ
    sort = jnp.where(r_in == (r_out % per) * NZ + r_out // per, 1.0, 0.0).astype(BF16)

    def unfold(i, carry):
        piece = thin[pl.ds(i * NZ, NZ)].reshape(block, part)
        piece = jnp.dot(sort, piece, preferred_element_type=F32).astype(BF16)
        for k in range(NZ):
            chosen[pl.ds(pl.multiple_of(i * per, per), per), k * part : (k + 1) * part] = piece[k * per : (k + 1) * per]
        return carry

    lax.fori_loop(0, n_exp // NZ, unfold, 0)
    remote(wide, wide, wide_s, wide_r, me).wait_recv()
    chosen[:, half:width] = flat(wide)

    def activate(k, index):
        both = dot_nt(gate_up[pl.ds(pl.multiple_of(index * 2 * units, 2 * units), 2 * units), :], chosen[...])
        gate, upper = both[0:units], both[units : 2 * units]
        mine = at(act, (z * NX + index) * units, units, units)
        mine[...] = (gate / (1.0 + jnp.exp(-gate)) * upper).astype(BF16)
        for d in range(1, NZ):
            remote(mine, mine, act_s.at[k, d], act_r.at[k, z], (z_peer(d), e)).start()

    order = (x, x_left, x_right, far)
    activate(0, x)
    remote(up_of(x_left), up_of(x_left), w_s.at[1], w_r.at[1], me).wait_recv()
    activate(1, x_left)
    remote(gate_of(x_right), gate_of(x_right), w_s.at[3], w_r.at[3], me).wait_recv()
    activate(2, x_right)

    for copy in (g_right, u_right, u_left, g_left, g_on, u_on):
        copy.wait_send()
    own[2].wait()
    d_right = remote(down_of(x), down_of(x), w_s.at[6], w_r.at[6], right)
    d_left = remote(down_of(x), down_of(x), w_s.at[7], w_r.at[7], left)
    d_right.start()
    d_left.start()
    remote(gate_of(far), gate_of(far), w_s.at[4], w_r.at[4], me).wait_recv()
    remote(up_of(far), up_of(far), w_s.at[5], w_r.at[5], me).wait_recv()
    activate(3, far)
    for k in range(NX):
        for d in range(1, NZ):
            p = (z + d) % NZ
            theirs = at(act, (p * NX + order[k]) * units, units, units)
            remote(theirs, theirs, act_s.at[k, d], act_r.at[k, p], me).wait_recv()

    def project(k, index):
        y = jnp.dot(down_w[pl.ds(pl.multiple_of(index * cols, cols), cols), :], act[...], preferred_element_type=F32)
        y_send[k] = jnp.transpose(y, (1, 0)).reshape(y_send.shape[1:]).astype(BF16)

        def send_y(d, carry):
            peer = lax.rem(e + d, n_exp)
            remote(y_send.at[k, peer], y_recv.at[k, e], y_s.at[k], y_r.at[k], (c, peer)).start()
            return carry

        pltpu.make_async_copy(y_send.at[k, e], y_recv.at[k, e], y_r.at[k]).start()
        lax.fori_loop(1, n_exp, send_y, 0)

    combine = jnp.concatenate([table[i, 0:tok, :] for i in range(NZ)], axis=0)
    high = combine.astype(BF16)
    rest = (combine - high.astype(F32)).astype(BF16)

    def gather(k, index):
        remote(y_recv.at[k], y_recv.at[k], y_s.at[k], y_r.at[k], me).wait_recv()
        arrived = flat(y_recv.at[k])
        total = jnp.dot(high, arrived, preferred_element_type=F32)
        total = total + jnp.dot(rest, arrived, preferred_element_type=F32)
        mixed[k] = total.reshape(mixed.shape[1:]).astype(BF16)
        for d in range(1, NZ):
            p = (z + d) % NZ
            remote(mixed.at[k, p], final.at[z, index], fin_s.at[k, d], fin_r.at[k, z], (z_peer(d), e)).start()
        final[z, index] = mixed[k, z]

    project(0, x)
    remote(down_of(x_left), down_of(x_left), w_s.at[6], w_r.at[6], me).wait_recv()
    f_right = remote(down_part(x_left, 0), down_part(x_left, 0), w_s.at[8], w_r.at[8], right)
    f_right.start()
    remote(down_of(x_right), down_of(x_right), w_s.at[7], w_r.at[7], me).wait_recv()
    f_left = remote(down_part(x_right, 1), down_part(x_right, 1), w_s.at[9], w_r.at[9], left)
    f_left.start()
    project(1, x_left)
    project(2, x_right)
    gather(0, x)
    remote(down_part(far, 0), down_part(far, 0), w_s.at[8], w_r.at[8], me).wait_recv()
    remote(down_part(far, 1), down_part(far, 1), w_s.at[9], w_r.at[9], me).wait_recv()
    project(3, far)
    gather(1, x_left)
    gather(2, x_right)
    gather(3, far)
    for k in range(NX):
        for d in range(1, NZ):
            p = (z + d) % NZ
            remote(mixed.at[k, p], final.at[p, order[k]], fin_s.at[k, d], fin_r.at[k, p], me).wait_recv()
    pieces = [final[i // NX, i % NX].astype(F32) for i in range(n_ctx)]
    out_ref[0] = jnp.concatenate(pieces, axis=1).astype(BF16)

    lat_copy.wait_send()
    for d in range(1, NZ):
        remote(own_table, table.at[z], table_s.at[d], table_r.at[z], me).wait_send()
        remote(second, tokens.at[z], tok_s.at[d], tok_r.at[z], me).wait_send()
        remote(column, column, spread_s.at[d], spread_r.at[z], me).wait_send()
        for k in range(NX):
            mine = at(act, (z * NX + order[k]) * units, units, units)
            remote(mine, mine, act_s.at[k, d], act_r.at[k, z], me).wait_send()
            remote(mixed.at[k, 0], final.at[z, 0], fin_s.at[k, d], fin_r.at[k, z], me).wait_send()
    for copy in (d_right, d_left, f_right, f_left):
        copy.wait_send()
    others = pl.ds(0, n_exp - 1)
    remote(thin_send.at[others], thin_send.at[others], thin_s, thin_r, me).wait_send()
    remote(wide_send.at[others], wide_send.at[others], wide_s, wide_r, me).wait_send()
    for k in range(NX):
        remote(y_send.at[k, others], y_send.at[k, others], y_s.at[k], y_r.at[k], me).wait_send()


def on_device(hidden, queries, latents, expert_ids, route_weight, w_gate, w_up, w_down):
    n_exp = lax.axis_size("exp")
    tok, width = hidden.shape[1:]
    units, hid = w_gate.shape[1], w_down.shape[2]
    cols = w_down.shape[1]
    chunk = NZ * CAP
    slots = n_exp * chunk
    half = width // 2
    heads = queries.shape[1] // (LATENT + ROPE)
    dma = pltpu.SemaphoreType.DMA
    vmem = pl.BlockSpec(memory_space=pltpu.VMEM)
    hbm = pl.BlockSpec(memory_space=pltpu.HBM)
    moe_out, attended = pl.pallas_call(
        functools.partial(moe_kernel, n_exp),
        out_shape=(
            jax.ShapeDtypeStruct(hidden.shape, BF16),
            jax.ShapeDtypeStruct((queries.shape[0], heads * LATENT), BF16),
        ),
        in_specs=[vmem, vmem, vmem, vmem, vmem, hbm, hbm, hbm],
        out_specs=(vmem, vmem),
        scratch_shapes=[
            pltpu.VMEM(latents.shape, BF16),
            pltpu.VMEM((NZ, tok, half), BF16),
            pltpu.VMEM((NZ, 2 * tok, slots), F32),
            pltpu.VMEM((2 * tok, slots), F32),
            pltpu.VMEM((n_exp, chunk, half // NZ), BF16),
            pltpu.VMEM((n_exp, NZ, chunk, half // NZ), BF16),
            pltpu.VMEM((n_exp, chunk, half), BF16),
            pltpu.VMEM((n_exp, chunk, half), BF16),
            pltpu.VMEM((slots, width), BF16),
            pltpu.VMEM((NX * 2 * units, width), BF16),
            pltpu.VMEM((NX * cols, hid), BF16),
            pltpu.VMEM((NZ * NX * units, slots), BF16),
            pltpu.VMEM((NX, n_exp, chunk, cols), BF16),
            pltpu.VMEM((NX, n_exp, chunk, cols), BF16),
            pltpu.VMEM((NX, NZ, tok, cols), BF16),
            pltpu.VMEM((NZ, NX, tok, cols), BF16),
            dma((3,)),
            dma, dma,
            dma((NZ,)), dma((NZ,)), dma((NZ,)), dma((NZ,)),
            dma, dma,
            dma((NZ,)), dma((NZ,)),
            dma, dma,
            dma((10,)), dma((10,)),
            dma((NX, NZ)), dma((NX, NZ)),
            dma((NX,)), dma((NX,)),
            dma((NX, NZ)), dma((NX, NZ)),
        ],
        compiler_params=pltpu.CompilerParams(
            collective_id=0, has_side_effects=True, vmem_limit_bytes=56 << 20
        ),
    )(hidden, expert_ids, route_weight, queries, latents, w_gate, w_up, w_down)
    return attended, moe_out


def solution(mesh):
    placed = (
        P("exp", "ctx", None),
        P("ctx", "exp"),
        P("ctx", None),
        P("exp", "ctx", None),
        P("exp", "ctx", None),
        P("exp", "ctx", None),
        P("exp", "ctx", None),
        P("exp", "ctx", None),
    )
    return jax.shard_map(
        on_device,
        mesh=mesh,
        in_specs=placed,
        out_specs=(P("ctx", "exp"), P("exp", "ctx", None)),
        check_vma=False,
    )
```

```python
import functools

import jax
import jax.numpy as jnp
from jax import lax
from jax.experimental import pallas as pl
from jax.experimental.pallas import tpu as pltpu
from jax.sharding import PartitionSpec as P

LATENT = 512
ROPE = 64
SCALE = 0.07216878364870322
NX = 4
NZ = 4
CAP = 2
MESH = pl.DeviceIdType.MESH
F32, BF16 = jnp.float32, jnp.bfloat16


def dot_nt(left, right):
    return lax.dot_general(left, right, (((1,), (1,)), ((), ())), preferred_element_type=F32)


def flat(ref):
    value = ref[...]
    return value.reshape(-1, value.shape[-1])


def moe_kernel(
    n_exp,
    tok_ref, pick_ref, weight_ref, q_ref, lat_ref, wg_ref, wu_ref, wd_ref, out_ref, att_ref,
    prev, tokens, table, own_table, thin_send, thin, wide_send, wide, chosen, gate_up, down_w, act,
    y_send, y_recv, mixed, final,
    local_sem, lat_s, lat_r, tok_s, tok_r, table_s, table_r, thin_s, thin_r, spread_s, spread_r, wide_s, wide_r,
    w_s, w_r, act_s, act_r, y_s, y_r, fin_s, fin_r,
):
    c, e = lax.axis_index("ctx"), lax.axis_index("exp")
    n_ctx = NX * NZ
    z, x = c // NX, c % NX
    tok, width = tok_ref.shape[1], tok_ref.shape[2]
    units, cols = wg_ref.shape[1], wd_ref.shape[1]
    chunk = NZ * CAP
    slots = n_exp * chunk
    half = width // 2
    part = half // NZ
    x_left, x_right, far = (x + NX - 1) % NX, (x + 1) % NX, (x + 2) % NX
    right, left = (z * NX + x_right, e), (z * NX + x_left, e)
    after, before = (lax.rem(c + 1, n_ctx), e), (lax.rem(c + n_ctx - 1, n_ctx), e)
    me = (c, e)

    def z_peer(d):
        return ((z + d) % NZ) * NX + x

    def at(ref, start, size, step):
        return ref.at[pl.ds(pl.multiple_of(start, step), size), :]

    def gate_of(index):
        return at(gate_up, index * 2 * units, units, units)

    def up_of(index):
        return at(gate_up, index * 2 * units + units, units, units)

    def down_of(index):
        return at(down_w, index * cols, cols, cols)

    def down_part(index, k):
        return at(down_w, index * cols + k * (cols // 2), cols // 2, cols // 2)

    def remote(src, dst, send, recv, peer):
        return pltpu.make_async_remote_copy(
            src_ref=src, dst_ref=dst, send_sem=send, recv_sem=recv, device_id=peer, device_id_type=MESH
        )

    own = [
        pltpu.make_async_copy(src.at[0], dst, local_sem.at[i])
        for i, (src, dst) in enumerate(((wg_ref, gate_of(x)), (wu_ref, up_of(x)), (wd_ref, down_of(x))))
    ]
    for copy in own:
        copy.start()

    barrier = pltpu.get_barrier_semaphore()
    for peer in [left, right, before, after] + [(z_peer(d), e) for d in range(1, NZ)]:
        pl.semaphore_signal(barrier, inc=1, device_id=peer, device_id_type=MESH)

    def greet(d, carry):
        pl.semaphore_signal(barrier, inc=1, device_id=(c, lax.rem(e + d, n_exp)), device_id_type=MESH)
        return carry

    lax.fori_loop(1, n_exp, greet, 0)

    slot = lax.broadcasted_iota(jnp.int32, (slots, tok), 0)
    slot_expert, inner = slot // chunk, slot % chunk
    named = jnp.zeros((slots, tok), F32)
    coef = jnp.zeros((slots, tok), F32)
    for k in range(pick_ref.shape[0]):
        hit = pick_ref[k] == slot_expert
        named = jnp.where(hit, 1.0, named)
        coef = jnp.where(hit, weight_ref[k], coef)
    upper = lax.broadcasted_iota(jnp.int32, (tok, tok), 0) < lax.broadcasted_iota(jnp.int32, (tok, tok), 1)
    rank = jnp.dot(named, jnp.where(upper, 1.0, 0.0), preferred_element_type=F32)
    here = (inner // CAP == z) & (rank == (inner % CAP).astype(F32))
    both = jnp.concatenate([jnp.where(here, coef, 0.0), jnp.where(here, named, 0.0)], axis=1)
    own_table[...] = jnp.transpose(both, (1, 0))
    taken = jnp.where(rank == (inner // NZ).astype(F32), named, 0.0)
    thin_pick = jnp.concatenate([jnp.where(inner % NZ == k, taken, 0.0) for k in range(NZ)], axis=1).astype(BF16)
    first = tok_ref[0, :, 0:half].astype(F32)
    first = jnp.concatenate([first[:, k * part : (k + 1) * part] for k in range(NZ)], axis=0).astype(BF16)
    thin_send[...] = jnp.dot(thin_pick, first, preferred_element_type=F32).reshape(thin_send.shape).astype(BF16)

    own[0].wait()
    own[1].wait()
    pl.semaphore_wait(barrier, n_exp - 1 + NZ - 1 + 4)

    g_right = remote(gate_of(x), gate_of(x), w_s.at[0], w_r.at[0], right)
    u_right = remote(up_of(x), up_of(x), w_s.at[1], w_r.at[1], right)
    u_left = remote(up_of(x), up_of(x), w_s.at[2], w_r.at[2], left)
    g_left = remote(gate_of(x), gate_of(x), w_s.at[3], w_r.at[3], left)
    for copy in (g_right, u_left, u_right, g_left):
        copy.start()

    second = tok_ref.at[0, :, pl.ds(half, half)]
    for d in range(1, NZ):
        remote(own_table, table.at[z], table_s.at[d], table_r.at[z], (z_peer(d), e)).start()
        remote(second, tokens.at[z], tok_s.at[d], tok_r.at[z], (z_peer(d), e)).start()
    tokens[z] = tok_ref[0, :, half:width]
    table[z] = own_table[...]

    def thin_copy(peer):
        return remote(thin_send.at[peer], thin.at[e, z], thin_s, thin_r, (c, peer))

    def send_thin(d, carry):
        thin_copy(lax.rem(e + d, n_exp)).start()
        return carry

    pltpu.make_async_copy(thin_send.at[e], thin.at[e, z], thin_r).start()
    lax.fori_loop(1, n_exp, send_thin, 0)
    lat_copy = remote(lat_ref, prev, lat_s, lat_r, after)
    lat_copy.start()

    for d in range(1, NZ):
        p = (z + d) % NZ
        remote(own_table, table.at[p], table_s.at[d], table_r.at[p], me).wait_recv()
        remote(second, tokens.at[p], tok_s.at[d], tok_r.at[p], me).wait_recv()

    select = jnp.concatenate([table[i, tok : 2 * tok, :] for i in range(NZ)], axis=0)
    select = jnp.transpose(select, (1, 0)).astype(BF16)
    wide_send[...] = jnp.dot(select, flat(tokens), preferred_element_type=F32).reshape(wide_send.shape).astype(BF16)

    def send_wide(d, carry):
        peer = lax.rem(e + d, n_exp)
        remote(wide_send.at[peer], wide.at[e], wide_s, wide_r, (c, peer)).start()
        return carry

    pltpu.make_async_copy(wide_send.at[e], wide.at[e], wide_r).start()
    lax.fori_loop(1, n_exp, send_wide, 0)

    column = thin.at[:, z]
    remote(column, column, thin_s, thin_r, me).wait_recv()
    for d in (1, NZ - 1):
        remote(column, column, spread_s.at[d], spread_r.at[d], (z_peer(d), e)).start()

    lat_copy.wait_recv()
    n_att = lat_ref.shape[1]
    row = lax.broadcasted_iota(jnp.int32, (n_att, n_att), 0)
    col = lax.broadcasted_iota(jnp.int32, (n_att, n_att), 1)
    low = jnp.float32(-1e30)
    depth = LATENT + ROPE
    for h in range(q_ref.shape[1] // depth):
        query = q_ref[:, h * depth : (h + 1) * depth]
        s_own = jnp.where(col <= row, jnp.dot(query, lat_ref[...], preferred_element_type=F32) * SCALE, low)
        s_prev = jnp.where(c > 0, jnp.dot(query, prev[...], preferred_element_type=F32) * SCALE, low)
        top = jnp.maximum(jnp.max(s_own, axis=1, keepdims=True), jnp.max(s_prev, axis=1, keepdims=True))
        e_own, e_prev = jnp.exp(s_own - top), jnp.exp(s_prev - top)
        total = jnp.sum(e_own, axis=1, keepdims=True) + jnp.sum(e_prev, axis=1, keepdims=True)
        value = dot_nt((e_own / total).astype(BF16), lat_ref[0:LATENT, :])
        value = value + dot_nt((e_prev / total).astype(BF16), prev[0:LATENT, :])
        att_ref[:, h * LATENT : (h + 1) * LATENT] = value.astype(BF16)

    z_down, z_up, z_far = (z + NZ - 1) % NZ, (z + 1) % NZ, (z + 2) % NZ
    above, below = (z_peer(1), e), (z_peer(NZ - 1), e)

    def thin_half(index, k):
        return thin.at[pl.ds(k * (n_exp // 2), n_exp // 2), index]

    remote(thin.at[:, z_down], thin.at[:, z_down], spread_s.at[1], spread_r.at[1], me).wait_recv()
    t_up = remote(thin_half(z_down, 0), thin_half(z_down, 0), spread_s.at[0], spread_r.at[0], above)
    t_up.start()
    remote(thin.at[:, z_up], thin.at[:, z_up], spread_s.at[3], spread_r.at[3], me).wait_recv()
    t_down = remote(thin_half(z_up, 1), thin_half(z_up, 1), spread_s.at[2], spread_r.at[2], below)
    t_down.start()

    remote(gate_of(x_left), gate_of(x_left), w_s.at[0], w_r.at[0], me).wait_recv()
    g_on = remote(gate_of(x_left), gate_of(x_left), w_s.at[4], w_r.at[4], right)
    g_on.start()
    remote(up_of(x_right), up_of(x_right), w_s.at[2], w_r.at[2], me).wait_recv()
    u_on = remote(up_of(x_right), up_of(x_right), w_s.at[5], w_r.at[5], left)
    u_on.start()

    remote(thin_half(z_far, 0), thin_half(z_far, 0), spread_s.at[0], spread_r.at[0], me).wait_recv()
    remote(thin_half(z_far, 1), thin_half(z_far, 1), spread_s.at[2], spread_r.at[2], me).wait_recv()
    block = NZ * chunk * NZ
    r_out = lax.broadcasted_iota(jnp.int32, (block, block), 0)
    r_in = lax.broadcasted_iota(jnp.int32, (block, block), 1)
    per = block // NZ
    sort = jnp.where(r_in == (r_out % per) * NZ + r_out // per, 1.0, 0.0).astype(BF16)

    def unfold(i, carry):
        piece = thin[pl.ds(i * NZ, NZ)].reshape(block, part)
        piece = jnp.dot(sort, piece, preferred_element_type=F32).astype(BF16)
        for k in range(NZ):
            chosen[pl.ds(pl.multiple_of(i * per, per), per), k * part : (k + 1) * part] = piece[k * per : (k + 1) * per]
        return carry

    lax.fori_loop(0, n_exp // NZ, unfold, 0)
    remote(wide, wide, wide_s, wide_r, me).wait_recv()
    chosen[:, half:width] = flat(wide)

    def activate(k, index):
        both = dot_nt(gate_up[pl.ds(pl.multiple_of(index * 2 * units, 2 * units), 2 * units), :], chosen[...])
        gate, upper = both[0:units], both[units : 2 * units]
        mine = at(act, (z * NX + index) * units, units, units)
        mine[...] = (gate / (1.0 + jnp.exp(-gate)) * upper).astype(BF16)
        remote(mine, mine, act_s.at[k, 1], act_r.at[k, 1], above).start()
        remote(mine, mine, act_s.at[k, 3], act_r.at[k, 3], below).start()

    def act_of(z_index, k):
        return at(act, (z_index * NX + order[k]) * units, units, units)

    def act_half(z_index, k, j):
        return at(act, (z_index * NX + order[k]) * units + j * (units // 2), units // 2, units // 2)

    def pass_on(k):
        remote(act_of(z_down, k), act_of(z_down, k), act_s.at[k, 1], act_r.at[k, 1], me).wait_recv()
        remote(act_half(z_down, k, 0), act_half(z_down, k, 0), act_s.at[k, 0], act_r.at[k, 0], above).start()
        remote(act_of(z_up, k), act_of(z_up, k), act_s.at[k, 3], act_r.at[k, 3], me).wait_recv()
        remote(act_half(z_up, k, 1), act_half(z_up, k, 1), act_s.at[k, 2], act_r.at[k, 2], below).start()

    order = (x, x_left, x_right, far)
    activate(0, x)
    remote(up_of(x_left), up_of(x_left), w_s.at[1], w_r.at[1], me).wait_recv()
    activate(1, x_left)
    remote(gate_of(x_right), gate_of(x_right), w_s.at[3], w_r.at[3], me).wait_recv()
    activate(2, x_right)
    for k in range(3):
        pass_on(k)

    for copy in (g_right, u_right, u_left, g_left, g_on, u_on):
        copy.wait_send()
    own[2].wait()
    d_right = remote(down_of(x), down_of(x), w_s.at[6], w_r.at[6], right)
    d_left = remote(down_of(x), down_of(x), w_s.at[7], w_r.at[7], left)
    d_right.start()
    d_left.start()
    remote(gate_of(far), gate_of(far), w_s.at[4], w_r.at[4], me).wait_recv()
    remote(up_of(far), up_of(far), w_s.at[5], w_r.at[5], me).wait_recv()
    activate(3, far)
    pass_on(3)
    for k in range(NX):
        remote(act_half(z_far, k, 0), act_half(z_far, k, 0), act_s.at[k, 0], act_r.at[k, 0], me).wait_recv()
        remote(act_half(z_far, k, 1), act_half(z_far, k, 1), act_s.at[k, 2], act_r.at[k, 2], me).wait_recv()

    def project(k, index):
        y = jnp.dot(down_w[pl.ds(pl.multiple_of(index * cols, cols), cols), :], act[...], preferred_element_type=F32)
        y_send[k] = jnp.transpose(y, (1, 0)).reshape(y_send.shape[1:]).astype(BF16)

        def send_y(d, carry):
            peer = lax.rem(e + d, n_exp)
            remote(y_send.at[k, peer], y_recv.at[k, e], y_s.at[k], y_r.at[k], (c, peer)).start()
            return carry

        pltpu.make_async_copy(y_send.at[k, e], y_recv.at[k, e], y_r.at[k]).start()
        lax.fori_loop(1, n_exp, send_y, 0)

    combine = jnp.concatenate([table[i, 0:tok, :] for i in range(NZ)], axis=0)
    high = combine.astype(BF16)
    rest = (combine - high.astype(F32)).astype(BF16)

    def gather(k, index):
        remote(y_recv.at[k], y_recv.at[k], y_s.at[k], y_r.at[k], me).wait_recv()
        arrived = flat(y_recv.at[k])
        total = jnp.dot(high, arrived, preferred_element_type=F32)
        total = total + jnp.dot(rest, arrived, preferred_element_type=F32)
        mixed[k] = total.reshape(mixed.shape[1:]).astype(BF16)
        for d in range(1, NZ):
            p = (z + d) % NZ
            remote(mixed.at[k, p], final.at[z, index], fin_s.at[k, d], fin_r.at[k, z], (z_peer(d), e)).start()
        final[z, index] = mixed[k, z]

    project(0, x)
    remote(down_of(x_left), down_of(x_left), w_s.at[6], w_r.at[6], me).wait_recv()
    f_right = remote(down_part(x_left, 0), down_part(x_left, 0), w_s.at[8], w_r.at[8], right)
    f_right.start()
    remote(down_of(x_right), down_of(x_right), w_s.at[7], w_r.at[7], me).wait_recv()
    f_left = remote(down_part(x_right, 1), down_part(x_right, 1), w_s.at[9], w_r.at[9], left)
    f_left.start()
    project(1, x_left)
    project(2, x_right)
    gather(0, x)
    remote(down_part(far, 0), down_part(far, 0), w_s.at[8], w_r.at[8], me).wait_recv()
    remote(down_part(far, 1), down_part(far, 1), w_s.at[9], w_r.at[9], me).wait_recv()
    project(3, far)
    gather(1, x_left)
    gather(2, x_right)
    gather(3, far)
    for k in range(NX):
        for d in range(1, NZ):
            p = (z + d) % NZ
            remote(mixed.at[k, p], final.at[p, order[k]], fin_s.at[k, d], fin_r.at[k, p], me).wait_recv()
    pieces = [final[i // NX, i % NX].astype(F32) for i in range(n_ctx)]
    out_ref[0] = jnp.concatenate(pieces, axis=1).astype(BF16)

    lat_copy.wait_send()
    for d in range(1, NZ):
        remote(own_table, table.at[z], table_s.at[d], table_r.at[z], me).wait_send()
        remote(second, tokens.at[z], tok_s.at[d], tok_r.at[z], me).wait_send()
        for k in range(NX):
            remote(mixed.at[k, 0], final.at[z, 0], fin_s.at[k, d], fin_r.at[k, z], me).wait_send()
    for copy in (d_right, d_left, f_right, f_left, t_up, t_down):
        copy.wait_send()
    for d in (1, NZ - 1):
        remote(column, column, spread_s.at[d], spread_r.at[d], me).wait_send()
    for k in range(NX):
        for j, part_of in ((1, act_of(z, k)), (3, act_of(z, k)), (0, act_half(z_down, k, 0)), (2, act_half(z_up, k, 1))):
            remote(part_of, part_of, act_s.at[k, j], act_r.at[k, j], me).wait_send()
    others = pl.ds(0, n_exp - 1)
    remote(thin_send.at[others], thin_send.at[others], thin_s, thin_r, me).wait_send()
    remote(wide_send.at[others], wide_send.at[others], wide_s, wide_r, me).wait_send()
    for k in range(NX):
        remote(y_send.at[k, others], y_send.at[k, others], y_s.at[k], y_r.at[k], me).wait_send()


def on_device(hidden, queries, latents, expert_ids, route_weight, w_gate, w_up, w_down):
    n_exp = lax.axis_size("exp")
    tok, width = hidden.shape[1:]
    units, hid = w_gate.shape[1], w_down.shape[2]
    cols = w_down.shape[1]
    chunk = NZ * CAP
    slots = n_exp * chunk
    half = width // 2
    heads = queries.shape[1] // (LATENT + ROPE)
    dma = pltpu.SemaphoreType.DMA
    vmem = pl.BlockSpec(memory_space=pltpu.VMEM)
    hbm = pl.BlockSpec(memory_space=pltpu.HBM)
    moe_out, attended = pl.pallas_call(
        functools.partial(moe_kernel, n_exp),
        out_shape=(
            jax.ShapeDtypeStruct(hidden.shape, BF16),
            jax.ShapeDtypeStruct((queries.shape[0], heads * LATENT), BF16),
        ),
        in_specs=[vmem, vmem, vmem, vmem, vmem, hbm, hbm, hbm],
        out_specs=(vmem, vmem),
        scratch_shapes=[
            pltpu.VMEM(latents.shape[::-1], BF16),
            pltpu.VMEM((NZ, tok, half), BF16),
            pltpu.VMEM((NZ, 2 * tok, slots), F32),
            pltpu.VMEM((2 * tok, slots), F32),
            pltpu.VMEM((n_exp, chunk, half // NZ), BF16),
            pltpu.VMEM((n_exp, NZ, chunk, half // NZ), BF16),
            pltpu.VMEM((n_exp, chunk, half), BF16),
            pltpu.VMEM((n_exp, chunk, half), BF16),
            pltpu.VMEM((slots, width), BF16),
            pltpu.VMEM((NX * 2 * units, width), BF16),
            pltpu.VMEM((NX * cols, hid), BF16),
            pltpu.VMEM((NZ * NX * units, slots), BF16),
            pltpu.VMEM((NX, n_exp, chunk, cols), BF16),
            pltpu.VMEM((NX, n_exp, chunk, cols), BF16),
            pltpu.VMEM((NX, NZ, tok, cols), BF16),
            pltpu.VMEM((NZ, NX, tok, cols), BF16),
            dma((3,)),
            dma, dma,
            dma((NZ,)), dma((NZ,)), dma((NZ,)), dma((NZ,)),
            dma, dma,
            dma((NZ,)), dma((NZ,)),
            dma, dma,
            dma((10,)), dma((10,)),
            dma((NX, NZ)), dma((NX, NZ)),
            dma((NX,)), dma((NX,)),
            dma((NX, NZ)), dma((NX, NZ)),
        ],
        compiler_params=pltpu.CompilerParams(
            collective_id=0, has_side_effects=True, vmem_limit_bytes=56 << 20
        ),
    )(hidden, jnp.transpose(expert_ids, (2, 0, 1)), jnp.transpose(route_weight, (2, 0, 1)), queries, latents.T, w_gate, w_up, w_down)
    return attended, moe_out


def solution(mesh):
    placed = (
        P("exp", "ctx", None),
        P("ctx", "exp"),
        P("ctx", None),
        P("exp", "ctx", None),
        P("exp", "ctx", None),
        P("exp", "ctx", None),
        P("exp", "ctx", None),
        P("exp", "ctx", None),
    )
    return jax.shard_map(
        on_device,
        mesh=mesh,
        in_specs=placed,
        out_specs=(P("ctx", "exp"), P("exp", "ctx", None)),
        check_vma=False,
    )
```

```python
import functools

import jax
import jax.numpy as jnp
from jax import lax
from jax.experimental import pallas as pl
from jax.experimental.pallas import tpu as pltpu
from jax.sharding import PartitionSpec as P

LATENT = 512
ROPE = 64
SCALE = 0.07216878364870322
NX = 4
NZ = 4
CAP = 2
MESH = pl.DeviceIdType.MESH
F32, BF16 = jnp.float32, jnp.bfloat16


def dot_nt(left, right):
    return lax.dot_general(left, right, (((1,), (1,)), ((), ())), preferred_element_type=F32)


def flat(ref):
    value = ref[...]
    return value.reshape(-1, value.shape[-1])


def moe_kernel(
    n_exp,
    tok_ref, pick_ref, weight_ref, q_ref, lat_ref, wg_ref, wu_ref, wd_ref, out_ref, att_ref,
    prev, tokens, table, own_table, thin_send, thin, wide_send, wide, chosen, gate_up, down_w, act,
    y_send, y_recv, mixed, final,
    local_sem, lat_s, lat_r, tok_s, tok_r, table_s, table_r, thin_s, thin_r, spread_s, spread_r, wide_s, wide_r,
    w_s, w_r, act_s, act_r, y_s, y_r, fin_s, fin_r,
):
    c, e = lax.axis_index("ctx"), lax.axis_index("exp")
    n_ctx = NX * NZ
    z, x = c // NX, c % NX
    tok, width = tok_ref.shape[1], tok_ref.shape[2]
    units, cols = wg_ref.shape[1], wd_ref.shape[1]
    chunk = NZ * CAP
    slots = n_exp * chunk
    part = thin.shape[-1]
    half = part * NZ
    x_left, x_right, far = (x + NX - 1) % NX, (x + 1) % NX, (x + 2) % NX
    right, left = (z * NX + x_right, e), (z * NX + x_left, e)
    after, before = (lax.rem(c + 1, n_ctx), e), (lax.rem(c + n_ctx - 1, n_ctx), e)
    me = (c, e)

    def z_peer(d):
        return ((z + d) % NZ) * NX + x

    def at(ref, start, size, step):
        return ref.at[pl.ds(pl.multiple_of(start, step), size), :]

    def gate_of(index):
        return at(gate_up, index * 2 * units, units, units)

    def up_of(index):
        return at(gate_up, index * 2 * units + units, units, units)

    def down_of(index):
        return at(down_w, index * cols, cols, cols)

    def down_part(index, k):
        return at(down_w, index * cols + k * (cols // 2), cols // 2, cols // 2)

    def remote(src, dst, send, recv, peer):
        return pltpu.make_async_remote_copy(
            src_ref=src, dst_ref=dst, send_sem=send, recv_sem=recv, device_id=peer, device_id_type=MESH
        )

    own = [
        pltpu.make_async_copy(src.at[0], dst, local_sem.at[i])
        for i, (src, dst) in enumerate(((wg_ref, gate_of(x)), (wu_ref, up_of(x)), (wd_ref, down_of(x))))
    ]
    for copy in own:
        copy.start()

    barrier = pltpu.get_barrier_semaphore()
    for peer in [left, right, before, after] + [(z_peer(d), e) for d in range(1, NZ)]:
        pl.semaphore_signal(barrier, inc=1, device_id=peer, device_id_type=MESH)

    def greet(d, carry):
        pl.semaphore_signal(barrier, inc=1, device_id=(c, lax.rem(e + d, n_exp)), device_id_type=MESH)
        return carry

    lax.fori_loop(1, n_exp, greet, 0)

    slot = lax.broadcasted_iota(jnp.int32, (slots, tok), 0)
    slot_expert, inner = slot // chunk, slot % chunk
    named = jnp.zeros((slots, tok), F32)
    coef = jnp.zeros((slots, tok), F32)
    for k in range(pick_ref.shape[0]):
        hit = pick_ref[k] == slot_expert
        named = jnp.where(hit, 1.0, named)
        coef = jnp.where(hit, weight_ref[k], coef)
    upper = lax.broadcasted_iota(jnp.int32, (tok, tok), 0) < lax.broadcasted_iota(jnp.int32, (tok, tok), 1)
    rank = jnp.dot(named, jnp.where(upper, 1.0, 0.0), preferred_element_type=F32)
    here = (inner // CAP == z) & (rank == (inner % CAP).astype(F32))
    both = jnp.concatenate([jnp.where(here, coef, 0.0), jnp.where(here, named, 0.0)], axis=1)
    own_table[...] = jnp.transpose(both, (1, 0))
    taken = jnp.where(rank == (inner // NZ).astype(F32), named, 0.0)
    thin_pick = jnp.concatenate([jnp.where(inner % NZ == k, taken, 0.0) for k in range(NZ)], axis=1).astype(BF16)
    first = tok_ref[0, :, 0:half].astype(F32)
    first = jnp.concatenate([first[:, k * part : (k + 1) * part] for k in range(NZ)], axis=0).astype(BF16)
    thin_send[...] = jnp.dot(thin_pick, first, preferred_element_type=F32).reshape(thin_send.shape).astype(BF16)

    own[0].wait()
    own[1].wait()
    pl.semaphore_wait(barrier, n_exp - 1 + NZ - 1 + 4)

    g_right = remote(gate_of(x), gate_of(x), w_s.at[0], w_r.at[0], right)
    u_right = remote(up_of(x), up_of(x), w_s.at[1], w_r.at[1], right)
    u_left = remote(up_of(x), up_of(x), w_s.at[2], w_r.at[2], left)
    g_left = remote(gate_of(x), gate_of(x), w_s.at[3], w_r.at[3], left)
    for copy in (g_right, u_left, u_right, g_left):
        copy.start()

    second = tok_ref.at[0, :, pl.ds(half, width - half)]
    for d in range(1, NZ):
        remote(own_table, table.at[z], table_s.at[d], table_r.at[z], (z_peer(d), e)).start()
        remote(second, tokens.at[z], tok_s.at[d], tok_r.at[z], (z_peer(d), e)).start()
    tokens[z] = tok_ref[0, :, half:width]
    table[z] = own_table[...]

    def thin_copy(peer):
        return remote(thin_send.at[peer], thin.at[e, z], thin_s, thin_r, (c, peer))

    def send_thin(d, carry):
        thin_copy(lax.rem(e + d, n_exp)).start()
        return carry

    pltpu.make_async_copy(thin_send.at[e], thin.at[e, z], thin_r).start()
    lax.fori_loop(1, n_exp, send_thin, 0)
    lat_copy = remote(lat_ref, prev, lat_s, lat_r, after)
    lat_copy.start()

    for d in range(1, NZ):
        p = (z + d) % NZ
        remote(own_table, table.at[p], table_s.at[d], table_r.at[p], me).wait_recv()
        remote(second, tokens.at[p], tok_s.at[d], tok_r.at[p], me).wait_recv()

    select = jnp.concatenate([table[i, tok : 2 * tok, :] for i in range(NZ)], axis=0)
    select = jnp.transpose(select, (1, 0)).astype(BF16)
    wide_send[...] = jnp.dot(select, flat(tokens), preferred_element_type=F32).reshape(wide_send.shape).astype(BF16)

    def send_wide(d, carry):
        peer = lax.rem(e + d, n_exp)
        remote(wide_send.at[peer], wide.at[e], wide_s, wide_r, (c, peer)).start()
        return carry

    pltpu.make_async_copy(wide_send.at[e], wide.at[e], wide_r).start()
    lax.fori_loop(1, n_exp, send_wide, 0)

    column = thin.at[:, z]
    remote(column, column, thin_s, thin_r, me).wait_recv()
    for d in (1, NZ - 1):
        remote(column, column, spread_s.at[d], spread_r.at[d], (z_peer(d), e)).start()

    remote(gate_of(x_left), gate_of(x_left), w_s.at[0], w_r.at[0], me).wait_recv()
    g_on = remote(gate_of(x_left), gate_of(x_left), w_s.at[4], w_r.at[4], right)
    g_on.start()
    remote(up_of(x_right), up_of(x_right), w_s.at[2], w_r.at[2], me).wait_recv()
    u_on = remote(up_of(x_right), up_of(x_right), w_s.at[5], w_r.at[5], left)
    u_on.start()

    own[2].wait()
    d_right = remote(down_part(x, 0), down_part(x, 0), w_s.at[6], w_r.at[6], right)
    d_left = remote(down_part(x, 1), down_part(x, 1), w_s.at[7], w_r.at[7], left)
    d_right_too = remote(down_part(x, 1), down_part(x, 1), w_s.at[10], w_r.at[10], right)
    d_left_too = remote(down_part(x, 0), down_part(x, 0), w_s.at[11], w_r.at[11], left)
    for copy in (d_right, d_left, d_right_too, d_left_too):
        copy.start()

    z_down, z_up, z_far = (z + NZ - 1) % NZ, (z + 1) % NZ, (z + 2) % NZ
    above, below = (z_peer(1), e), (z_peer(NZ - 1), e)

    def thin_half(index, k):
        return thin.at[pl.ds(k * (n_exp // 2), n_exp // 2), index]

    remote(thin.at[:, z_down], thin.at[:, z_down], spread_s.at[1], spread_r.at[1], me).wait_recv()
    t_up = remote(thin_half(z_down, 0), thin_half(z_down, 0), spread_s.at[0], spread_r.at[0], above)
    t_up.start()
    remote(thin.at[:, z_up], thin.at[:, z_up], spread_s.at[3], spread_r.at[3], me).wait_recv()
    t_down = remote(thin_half(z_up, 1), thin_half(z_up, 1), spread_s.at[2], spread_r.at[2], below)
    t_down.start()

    lat_copy.wait_recv()
    n_att = lat_ref.shape[1]
    row = lax.broadcasted_iota(jnp.int32, (n_att, n_att), 0)
    col = lax.broadcasted_iota(jnp.int32, (n_att, n_att), 1)
    low = jnp.float32(-1e30)
    depth = LATENT + ROPE
    for h in range(q_ref.shape[1] // depth):
        query = q_ref[:, h * depth : (h + 1) * depth]
        s_own = jnp.where(col <= row, jnp.dot(query, lat_ref[...], preferred_element_type=F32) * SCALE, low)
        s_prev = jnp.where(c > 0, jnp.dot(query, prev[...], preferred_element_type=F32) * SCALE, low)
        top = jnp.maximum(jnp.max(s_own, axis=1, keepdims=True), jnp.max(s_prev, axis=1, keepdims=True))
        e_own, e_prev = jnp.exp(s_own - top), jnp.exp(s_prev - top)
        total = jnp.sum(e_own, axis=1, keepdims=True) + jnp.sum(e_prev, axis=1, keepdims=True)
        value = dot_nt((e_own / total).astype(BF16), lat_ref[0:LATENT, :])
        value = value + dot_nt((e_prev / total).astype(BF16), prev[0:LATENT, :])
        att_ref[:, h * LATENT : (h + 1) * LATENT] = value.astype(BF16)

    remote(thin_half(z_far, 0), thin_half(z_far, 0), spread_s.at[0], spread_r.at[0], me).wait_recv()
    remote(thin_half(z_far, 1), thin_half(z_far, 1), spread_s.at[2], spread_r.at[2], me).wait_recv()
    block = NZ * chunk * NZ
    r_out = lax.broadcasted_iota(jnp.int32, (block, block), 0)
    r_in = lax.broadcasted_iota(jnp.int32, (block, block), 1)
    per = block // NZ
    sort = jnp.where(r_in == (r_out % per) * NZ + r_out // per, 1.0, 0.0).astype(BF16)

    def unfold(i, carry):
        piece = thin[pl.ds(i * NZ, NZ)].reshape(block, part)
        piece = jnp.dot(sort, piece, preferred_element_type=F32).astype(BF16)
        for k in range(NZ):
            chosen[pl.ds(pl.multiple_of(i * per, per), per), k * part : (k + 1) * part] = piece[k * per : (k + 1) * per]
        return carry

    lax.fori_loop(0, n_exp // NZ, unfold, 0)
    remote(wide, wide, wide_s, wide_r, me).wait_recv()
    chosen[:, half:width] = flat(wide)

    def activate(k, index):
        both = dot_nt(gate_up[pl.ds(pl.multiple_of(index * 2 * units, 2 * units), 2 * units), :], chosen[...])
        gate, upper = both[0:units], both[units : 2 * units]
        mine = at(act, (z * NX + index) * units, units, units)
        mine[...] = (gate / (1.0 + jnp.exp(-gate)) * upper).astype(BF16)
        remote(mine, mine, act_s.at[k, 1], act_r.at[k, 1], above).start()
        remote(mine, mine, act_s.at[k, 3], act_r.at[k, 3], below).start()

    def act_of(z_index, k):
        return at(act, (z_index * NX + order[k]) * units, units, units)

    def act_half(z_index, k, j):
        return at(act, (z_index * NX + order[k]) * units + j * (units // 2), units // 2, units // 2)

    def pass_on(k):
        remote(act_of(z_down, k), act_of(z_down, k), act_s.at[k, 1], act_r.at[k, 1], me).wait_recv()
        remote(act_half(z_down, k, 0), act_half(z_down, k, 0), act_s.at[k, 0], act_r.at[k, 0], above).start()
        remote(act_of(z_up, k), act_of(z_up, k), act_s.at[k, 3], act_r.at[k, 3], me).wait_recv()
        remote(act_half(z_up, k, 1), act_half(z_up, k, 1), act_s.at[k, 2], act_r.at[k, 2], below).start()

    order = (x, x_left, x_right, far)
    activate(0, x)
    remote(up_of(x_left), up_of(x_left), w_s.at[1], w_r.at[1], me).wait_recv()
    activate(1, x_left)
    remote(gate_of(x_right), gate_of(x_right), w_s.at[3], w_r.at[3], me).wait_recv()
    activate(2, x_right)
    for k in range(3):
        pass_on(k)

    remote(gate_of(far), gate_of(far), w_s.at[4], w_r.at[4], me).wait_recv()
    remote(up_of(far), up_of(far), w_s.at[5], w_r.at[5], me).wait_recv()
    activate(3, far)
    pass_on(3)
    remote(down_part(x_left, 0), down_part(x_left, 0), w_s.at[6], w_r.at[6], me).wait_recv()
    f_right = remote(down_part(x_left, 0), down_part(x_left, 0), w_s.at[8], w_r.at[8], right)
    f_right.start()
    remote(down_part(x_right, 1), down_part(x_right, 1), w_s.at[7], w_r.at[7], me).wait_recv()
    f_left = remote(down_part(x_right, 1), down_part(x_right, 1), w_s.at[9], w_r.at[9], left)
    f_left.start()
    for k in range(NX):
        remote(act_half(z_far, k, 0), act_half(z_far, k, 0), act_s.at[k, 0], act_r.at[k, 0], me).wait_recv()
        remote(act_half(z_far, k, 1), act_half(z_far, k, 1), act_s.at[k, 2], act_r.at[k, 2], me).wait_recv()

    def project(k, index):
        y = jnp.dot(down_w[pl.ds(pl.multiple_of(index * cols, cols), cols), :], act[...], preferred_element_type=F32)
        y_send[k] = jnp.transpose(y, (1, 0)).reshape(y_send.shape[1:]).astype(BF16)

        def send_y(d, carry):
            peer = lax.rem(e + d, n_exp)
            remote(y_send.at[k, peer], y_recv.at[k, e], y_s.at[k], y_r.at[k], (c, peer)).start()
            return carry

        pltpu.make_async_copy(y_send.at[k, e], y_recv.at[k, e], y_r.at[k]).start()
        lax.fori_loop(1, n_exp, send_y, 0)

    combine = jnp.concatenate([table[i, 0:tok, :] for i in range(NZ)], axis=0)
    high = combine.astype(BF16)
    rest = (combine - high.astype(F32)).astype(BF16)

    def gather(k, index):
        remote(y_recv.at[k], y_recv.at[k], y_s.at[k], y_r.at[k], me).wait_recv()
        arrived = flat(y_recv.at[k])
        total = jnp.dot(high, arrived, preferred_element_type=F32)
        total = total + jnp.dot(rest, arrived, preferred_element_type=F32)
        mixed[k] = total.reshape(mixed.shape[1:]).astype(BF16)
        for d in range(1, NZ):
            p = (z + d) % NZ
            remote(mixed.at[k, p], final.at[z, index], fin_s.at[k, d], fin_r.at[k, z], (z_peer(d), e)).start()
        final[z, index] = mixed[k, z]

    project(0, x)
    remote(down_part(x_left, 1), down_part(x_left, 1), w_s.at[10], w_r.at[10], me).wait_recv()
    project(1, x_left)
    remote(down_part(x_right, 0), down_part(x_right, 0), w_s.at[11], w_r.at[11], me).wait_recv()
    project(2, x_right)
    remote(down_part(far, 0), down_part(far, 0), w_s.at[8], w_r.at[8], me).wait_recv()
    remote(down_part(far, 1), down_part(far, 1), w_s.at[9], w_r.at[9], me).wait_recv()
    project(3, far)
    gather(0, x)
    gather(1, x_left)
    gather(2, x_right)
    gather(3, far)
    for k in range(NX):
        for d in range(1, NZ):
            p = (z + d) % NZ
            remote(mixed.at[k, p], final.at[p, order[k]], fin_s.at[k, d], fin_r.at[k, p], me).wait_recv()
    pieces = [final[i // NX, i % NX].astype(F32) for i in range(n_ctx)]
    out_ref[0] = jnp.concatenate(pieces, axis=1).astype(BF16)

    lat_copy.wait_send()
    for d in range(1, NZ):
        remote(own_table, table.at[z], table_s.at[d], table_r.at[z], me).wait_send()
        remote(second, tokens.at[z], tok_s.at[d], tok_r.at[z], me).wait_send()
        for k in range(NX):
            remote(mixed.at[k, 0], final.at[z, 0], fin_s.at[k, d], fin_r.at[k, z], me).wait_send()
    for copy in (g_right, u_right, u_left, g_left, g_on, u_on, d_right, d_left, d_right_too, d_left_too, f_right, f_left, t_up, t_down):
        copy.wait_send()
    for d in (1, NZ - 1):
        remote(column, column, spread_s.at[d], spread_r.at[d], me).wait_send()
    for k in range(NX):
        for j, part_of in ((1, act_of(z, k)), (3, act_of(z, k)), (0, act_half(z_down, k, 0)), (2, act_half(z_up, k, 1))):
            remote(part_of, part_of, act_s.at[k, j], act_r.at[k, j], me).wait_send()
    others = pl.ds(0, n_exp - 1)
    remote(thin_send.at[others], thin_send.at[others], thin_s, thin_r, me).wait_send()
    remote(wide_send.at[others], wide_send.at[others], wide_s, wide_r, me).wait_send()
    for k in range(NX):
        remote(y_send.at[k, others], y_send.at[k, others], y_s.at[k], y_r.at[k], me).wait_send()


def on_device(hidden, queries, latents, expert_ids, route_weight, w_gate, w_up, w_down):
    n_exp = lax.axis_size("exp")
    tok, width = hidden.shape[1:]
    units, hid = w_gate.shape[1], w_down.shape[2]
    cols = w_down.shape[1]
    chunk = NZ * CAP
    slots = n_exp * chunk
    half = width // 2
    heads = queries.shape[1] // (LATENT + ROPE)
    dma = pltpu.SemaphoreType.DMA
    vmem = pl.BlockSpec(memory_space=pltpu.VMEM)
    hbm = pl.BlockSpec(memory_space=pltpu.HBM)
    moe_out, attended = pl.pallas_call(
        functools.partial(moe_kernel, n_exp),
        out_shape=(
            jax.ShapeDtypeStruct(hidden.shape, BF16),
            jax.ShapeDtypeStruct((queries.shape[0], heads * LATENT), BF16),
        ),
        in_specs=[vmem, vmem, vmem, vmem, vmem, hbm, hbm, hbm],
        out_specs=(vmem, vmem),
        scratch_shapes=[
            pltpu.VMEM(latents.shape[::-1], BF16),
            pltpu.VMEM((NZ, tok, width - half), BF16),
            pltpu.VMEM((NZ, 2 * tok, slots), F32),
            pltpu.VMEM((2 * tok, slots), F32),
            pltpu.VMEM((n_exp, chunk, half // NZ), BF16),
            pltpu.VMEM((n_exp, NZ, chunk, half // NZ), BF16),
            pltpu.VMEM((n_exp, chunk, width - half), BF16),
            pltpu.VMEM((n_exp, chunk, width - half), BF16),
            pltpu.VMEM((slots, width), BF16),
            pltpu.VMEM((NX * 2 * units, width), BF16),
            pltpu.VMEM((NX * cols, hid), BF16),
            pltpu.VMEM((NZ * NX * units, slots), BF16),
            pltpu.VMEM((NX, n_exp, chunk, cols), BF16),
            pltpu.VMEM((NX, n_exp, chunk, cols), BF16),
            pltpu.VMEM((NX, NZ, tok, cols), BF16),
            pltpu.VMEM((NZ, NX, tok, cols), BF16),
            dma((3,)),
            dma, dma,
            dma((NZ,)), dma((NZ,)), dma((NZ,)), dma((NZ,)),
            dma, dma,
            dma((NZ,)), dma((NZ,)),
            dma, dma,
            dma((12,)), dma((12,)),
            dma((NX, NZ)), dma((NX, NZ)),
            dma((NX,)), dma((NX,)),
            dma((NX, NZ)), dma((NX, NZ)),
        ],
        compiler_params=pltpu.CompilerParams(
            collective_id=0, has_side_effects=True, vmem_limit_bytes=56 << 20
        ),
    )(hidden, jnp.transpose(expert_ids, (2, 0, 1)), jnp.transpose(route_weight, (2, 0, 1)), queries, latents.T, w_gate, w_up, w_down)
    return attended, moe_out


def solution(mesh):
    placed = (
        P("exp", "ctx", None),
        P("ctx", "exp"),
        P("ctx", None),
        P("exp", "ctx", None),
        P("exp", "ctx", None),
        P("exp", "ctx", None),
        P("exp", "ctx", None),
        P("exp", "ctx", None),
    )
    return jax.shard_map(
        on_device,
        mesh=mesh,
        in_specs=placed,
        out_specs=(P("ctx", "exp"), P("exp", "ctx", None)),
        check_vma=False,
    )
```

```python
import functools

import jax
import jax.numpy as jnp
from jax import lax
from jax.experimental import pallas as pl
from jax.experimental.pallas import tpu as pltpu
from jax.sharding import PartitionSpec as P

LATENT = 512
ROPE = 64
SCALE = 0.07216878364870322
NX = 4
NZ = 4
CAP = 2
MESH = pl.DeviceIdType.MESH
F32, BF16 = jnp.float32, jnp.bfloat16


def dot_nt(left, right):
    return lax.dot_general(left, right, (((1,), (1,)), ((), ())), preferred_element_type=F32)


def flat(ref):
    value = ref[...]
    return value.reshape(-1, value.shape[-1])


def moe_kernel(
    n_exp,
    tok_ref, pick_ref, weight_ref, q_ref, lat_ref, wg_ref, wu_ref, wd_ref, out_ref, att_ref,
    prev, tokens, table, own_table, thin_send, thin, wide_send, wide, chosen, gate_up, down_w, act,
    y_send, y_recv, mixed, final,
    local_sem, lat_s, lat_r, tok_s, tok_r, table_s, table_r, thin_s, thin_r, spread_s, spread_r, wide_s, wide_r,
    w_s, w_r, act_s, act_r, y_s, y_r, fin_s, fin_r,
):
    c, e = lax.axis_index("ctx"), lax.axis_index("exp")
    n_ctx = NX * NZ
    z, x = c // NX, c % NX
    tok, width = tok_ref.shape[1], tok_ref.shape[2]
    units, cols = wg_ref.shape[1], wd_ref.shape[1]
    chunk = NZ * CAP
    slots = n_exp * chunk
    part = thin.shape[-1]
    half = part * NZ
    x_left, x_right, far = (x + NX - 1) % NX, (x + 1) % NX, (x + 2) % NX
    right, left = (z * NX + x_right, e), (z * NX + x_left, e)
    after, before = (lax.rem(c + 1, n_ctx), e), (lax.rem(c + n_ctx - 1, n_ctx), e)
    me = (c, e)

    def z_peer(d):
        return ((z + d) % NZ) * NX + x

    def at(ref, start, size, step):
        return ref.at[pl.ds(pl.multiple_of(start, step), size), :]

    def gate_of(index):
        return at(gate_up, index * 2 * units, units, units)

    def up_of(index):
        return at(gate_up, index * 2 * units + units, units, units)

    def down_of(index):
        return at(down_w, index * cols, cols, cols)

    def down_part(index, k):
        return at(down_w, index * cols + k * (cols // 2), cols // 2, cols // 2)

    def remote(src, dst, send, recv, peer):
        return pltpu.make_async_remote_copy(
            src_ref=src, dst_ref=dst, send_sem=send, recv_sem=recv, device_id=peer, device_id_type=MESH
        )

    own = [
        pltpu.make_async_copy(src.at[0], dst, local_sem.at[i])
        for i, (src, dst) in enumerate(((wg_ref, gate_of(x)), (wu_ref, up_of(x)), (wd_ref, down_of(x))))
    ]
    for copy in own:
        copy.start()

    barrier = pltpu.get_barrier_semaphore()
    for peer in [left, right, before, after] + [(z_peer(d), e) for d in range(1, NZ)]:
        pl.semaphore_signal(barrier, inc=1, device_id=peer, device_id_type=MESH)

    def greet(d, carry):
        pl.semaphore_signal(barrier, inc=1, device_id=(c, lax.rem(e + d, n_exp)), device_id_type=MESH)
        return carry

    lax.fori_loop(1, n_exp, greet, 0)

    slot = lax.broadcasted_iota(jnp.int32, (slots, tok), 0)
    slot_expert, inner = slot // chunk, slot % chunk
    named = jnp.zeros((slots, tok), F32)
    coef = jnp.zeros((slots, tok), F32)
    for k in range(pick_ref.shape[0]):
        hit = pick_ref[k] == slot_expert
        named = jnp.where(hit, 1.0, named)
        coef = jnp.where(hit, weight_ref[k], coef)
    upper = lax.broadcasted_iota(jnp.int32, (tok, tok), 0) < lax.broadcasted_iota(jnp.int32, (tok, tok), 1)
    rank = jnp.dot(named, jnp.where(upper, 1.0, 0.0), preferred_element_type=F32)
    here = (inner // CAP == z) & (rank == (inner % CAP).astype(F32))
    both = jnp.concatenate([jnp.where(here, coef, 0.0), jnp.where(here, named, 0.0)], axis=1)
    own_table[...] = jnp.transpose(both, (1, 0))
    taken = jnp.where(rank == (inner // NZ).astype(F32), named, 0.0)
    thin_pick = jnp.concatenate([jnp.where(inner % NZ == k, taken, 0.0) for k in range(NZ)], axis=1).astype(BF16)
    first = tok_ref[0, :, 0:half].astype(F32)
    first = jnp.concatenate([first[:, k * part : (k + 1) * part] for k in range(NZ)], axis=0).astype(BF16)
    thin_send[...] = jnp.dot(thin_pick, first, preferred_element_type=F32).reshape(thin_send.shape).astype(BF16)

    own[0].wait()
    own[1].wait()
    pl.semaphore_wait(barrier, n_exp - 1 + NZ - 1 + 4)

    g_right = remote(gate_of(x), gate_of(x), w_s.at[0], w_r.at[0], right)
    u_right = remote(up_of(x), up_of(x), w_s.at[1], w_r.at[1], right)
    u_left = remote(up_of(x), up_of(x), w_s.at[2], w_r.at[2], left)
    g_left = remote(gate_of(x), gate_of(x), w_s.at[3], w_r.at[3], left)
    for copy in (g_right, u_left, u_right, g_left):
        copy.start()

    second = tok_ref.at[0, :, pl.ds(half, width - half)]
    for d in range(1, NZ):
        remote(own_table, table.at[z], table_s.at[d], table_r.at[z], (z_peer(d), e)).start()
        remote(second, tokens.at[z], tok_s.at[d], tok_r.at[z], (z_peer(d), e)).start()
    tokens[z] = tok_ref[0, :, half:width]
    table[z] = own_table[...]

    def thin_copy(peer):
        return remote(thin_send.at[peer], thin.at[e, z], thin_s, thin_r, (c, peer))

    def send_thin(d, carry):
        thin_copy(lax.rem(e + d, n_exp)).start()
        return carry

    pltpu.make_async_copy(thin_send.at[e], thin.at[e, z], thin_r).start()
    lax.fori_loop(1, n_exp, send_thin, 0)
    lat_copy = remote(lat_ref, prev, lat_s, lat_r, after)
    lat_copy.start()

    for d in range(1, NZ):
        p = (z + d) % NZ
        remote(own_table, table.at[p], table_s.at[d], table_r.at[p], me).wait_recv()
        remote(second, tokens.at[p], tok_s.at[d], tok_r.at[p], me).wait_recv()

    select = jnp.concatenate([table[i, tok : 2 * tok, :] for i in range(NZ)], axis=0)
    select = jnp.transpose(select, (1, 0)).astype(BF16)
    wide_send[...] = jnp.dot(select, flat(tokens), preferred_element_type=F32).reshape(wide_send.shape).astype(BF16)

    def send_wide(d, carry):
        peer = lax.rem(e + d, n_exp)
        remote(wide_send.at[peer], wide.at[e], wide_s, wide_r, (c, peer)).start()
        return carry

    pltpu.make_async_copy(wide_send.at[e], wide.at[e], wide_r).start()
    lax.fori_loop(1, n_exp, send_wide, 0)

    column = thin.at[:, z]
    remote(column, column, thin_s, thin_r, me).wait_recv()
    for d in (1, NZ - 1):
        remote(column, column, spread_s.at[d], spread_r.at[d], (z_peer(d), e)).start()

    remote(gate_of(x_left), gate_of(x_left), w_s.at[0], w_r.at[0], me).wait_recv()
    g_on = remote(gate_of(x_left), gate_of(x_left), w_s.at[4], w_r.at[4], right)
    g_on.start()
    remote(up_of(x_right), up_of(x_right), w_s.at[2], w_r.at[2], me).wait_recv()
    u_on = remote(up_of(x_right), up_of(x_right), w_s.at[5], w_r.at[5], left)
    u_on.start()

    own[2].wait()
    d_right = remote(down_part(x, 0), down_part(x, 0), w_s.at[6], w_r.at[6], right)
    d_left = remote(down_part(x, 1), down_part(x, 1), w_s.at[7], w_r.at[7], left)
    d_right_too = remote(down_part(x, 1), down_part(x, 1), w_s.at[10], w_r.at[10], right)
    d_left_too = remote(down_part(x, 0), down_part(x, 0), w_s.at[11], w_r.at[11], left)
    for copy in (d_right, d_left, d_right_too, d_left_too):
        copy.start()

    z_down, z_up, z_far = (z + NZ - 1) % NZ, (z + 1) % NZ, (z + 2) % NZ
    above, below = (z_peer(1), e), (z_peer(NZ - 1), e)

    def thin_half(index, k):
        return thin.at[pl.ds(k * (n_exp // 2), n_exp // 2), index]

    remote(thin.at[:, z_down], thin.at[:, z_down], spread_s.at[1], spread_r.at[1], me).wait_recv()
    t_up = remote(thin_half(z_down, 0), thin_half(z_down, 0), spread_s.at[0], spread_r.at[0], above)
    t_up.start()
    remote(thin.at[:, z_up], thin.at[:, z_up], spread_s.at[3], spread_r.at[3], me).wait_recv()
    t_down = remote(thin_half(z_up, 1), thin_half(z_up, 1), spread_s.at[2], spread_r.at[2], below)
    t_down.start()

    lat_copy.wait_recv()
    n_att = lat_ref.shape[1]
    row = lax.broadcasted_iota(jnp.int32, (n_att, n_att), 0)
    col = lax.broadcasted_iota(jnp.int32, (n_att, n_att), 1)
    low = jnp.float32(-1e30)
    depth = LATENT + ROPE
    for h in range(q_ref.shape[1] // depth):
        query = q_ref[:, h * depth : (h + 1) * depth]
        s_own = jnp.where(col <= row, jnp.dot(query, lat_ref[...], preferred_element_type=F32) * SCALE, low)
        s_prev = jnp.where(c > 0, jnp.dot(query, prev[...], preferred_element_type=F32) * SCALE, low)
        top = jnp.maximum(jnp.max(s_own, axis=1, keepdims=True), jnp.max(s_prev, axis=1, keepdims=True))
        e_own, e_prev = jnp.exp(s_own - top), jnp.exp(s_prev - top)
        total = jnp.sum(e_own, axis=1, keepdims=True) + jnp.sum(e_prev, axis=1, keepdims=True)
        value = dot_nt((e_own / total).astype(BF16), lat_ref[0:LATENT, :])
        value = value + dot_nt((e_prev / total).astype(BF16), prev[0:LATENT, :])
        att_ref[:, h * LATENT : (h + 1) * LATENT] = value.astype(BF16)

    remote(thin_half(z_far, 0), thin_half(z_far, 0), spread_s.at[0], spread_r.at[0], me).wait_recv()
    remote(thin_half(z_far, 1), thin_half(z_far, 1), spread_s.at[2], spread_r.at[2], me).wait_recv()
    block = NZ * chunk * NZ
    r_out = lax.broadcasted_iota(jnp.int32, (block, block), 0)
    r_in = lax.broadcasted_iota(jnp.int32, (block, block), 1)
    per = block // NZ
    sort = jnp.where(r_in == (r_out % per) * NZ + r_out // per, 1.0, 0.0).astype(BF16)

    def unfold(i, carry):
        piece = thin[pl.ds(i * NZ, NZ)].reshape(block, part)
        piece = jnp.dot(sort, piece, preferred_element_type=F32).astype(BF16)
        for k in range(NZ):
            chosen[pl.ds(pl.multiple_of(i * per, per), per), k * part : (k + 1) * part] = piece[k * per : (k + 1) * per]
        return carry

    lax.fori_loop(0, n_exp // NZ, unfold, 0)
    remote(wide, wide, wide_s, wide_r, me).wait_recv()
    chosen[:, half:width] = flat(wide)

    def activate(k, index):
        both = dot_nt(gate_up[pl.ds(pl.multiple_of(index * 2 * units, 2 * units), 2 * units), :], chosen[...])
        gate, upper = both[0:units], both[units : 2 * units]
        mine = at(act, (z * NX + index) * units, units, units)
        mine[...] = (gate / (1.0 + jnp.exp(-gate)) * upper).astype(BF16)
        remote(mine, mine, act_s.at[k, 1], act_r.at[k, 1], above).start()
        remote(mine, mine, act_s.at[k, 3], act_r.at[k, 3], below).start()

    def act_of(z_index, k):
        return at(act, (z_index * NX + order[k]) * units, units, units)

    def act_half(z_index, k, j):
        return at(act, (z_index * NX + order[k]) * units + j * (units // 2), units // 2, units // 2)

    def pass_on(k):
        remote(act_of(z_down, k), act_of(z_down, k), act_s.at[k, 1], act_r.at[k, 1], me).wait_recv()
        remote(act_half(z_down, k, 0), act_half(z_down, k, 0), act_s.at[k, 0], act_r.at[k, 0], above).start()
        remote(act_of(z_up, k), act_of(z_up, k), act_s.at[k, 3], act_r.at[k, 3], me).wait_recv()
        remote(act_half(z_up, k, 1), act_half(z_up, k, 1), act_s.at[k, 2], act_r.at[k, 2], below).start()

    order = (x, x_left, x_right, far)
    activate(0, x)
    remote(up_of(x_left), up_of(x_left), w_s.at[1], w_r.at[1], me).wait_recv()
    activate(1, x_left)
    remote(gate_of(x_right), gate_of(x_right), w_s.at[3], w_r.at[3], me).wait_recv()
    activate(2, x_right)
    for k in range(3):
        pass_on(k)

    remote(gate_of(far), gate_of(far), w_s.at[4], w_r.at[4], me).wait_recv()
    remote(up_of(far), up_of(far), w_s.at[5], w_r.at[5], me).wait_recv()
    activate(3, far)
    pass_on(3)
    remote(down_part(x_left, 0), down_part(x_left, 0), w_s.at[6], w_r.at[6], me).wait_recv()
    f_right = remote(down_part(x_left, 0), down_part(x_left, 0), w_s.at[8], w_r.at[8], right)
    f_right.start()
    remote(down_part(x_right, 1), down_part(x_right, 1), w_s.at[7], w_r.at[7], me).wait_recv()
    f_left = remote(down_part(x_right, 1), down_part(x_right, 1), w_s.at[9], w_r.at[9], left)
    f_left.start()
    for k in range(NX):
        remote(act_half(z_far, k, 0), act_half(z_far, k, 0), act_s.at[k, 0], act_r.at[k, 0], me).wait_recv()
        remote(act_half(z_far, k, 1), act_half(z_far, k, 1), act_s.at[k, 2], act_r.at[k, 2], me).wait_recv()

    def project(k, index):
        y = jnp.dot(down_w[pl.ds(pl.multiple_of(index * cols, cols), cols), :], act[...], preferred_element_type=F32)
        y_send[k] = jnp.transpose(y, (1, 0)).reshape(y_send.shape[1:]).astype(BF16)

        def send_y(d, carry):
            peer = lax.rem(e + d, n_exp)
            remote(y_send.at[k, peer], y_recv.at[k, e], y_s.at[k], y_r.at[k], (c, peer)).start()
            return carry

        pltpu.make_async_copy(y_send.at[k, e], y_recv.at[k, e], y_r.at[k]).start()
        lax.fori_loop(1, n_exp, send_y, 0)

    combine = jnp.concatenate([table[i, 0:tok, :] for i in range(NZ)], axis=0)
    high = combine.astype(BF16)
    rest = (combine - high.astype(F32)).astype(BF16)

    def gather(k, index):
        remote(y_recv.at[k], y_recv.at[k], y_s.at[k], y_r.at[k], me).wait_recv()
        arrived = flat(y_recv.at[k])
        total = jnp.dot(high, arrived, preferred_element_type=F32)
        total = total + jnp.dot(rest, arrived, preferred_element_type=F32)
        mixed[k] = total.reshape(mixed.shape[1:]).astype(BF16)
        for d in range(1, NZ):
            p = (z + d) % NZ
            remote(mixed.at[k, p], final.at[z, index], fin_s.at[k, d], fin_r.at[k, z], (z_peer(d), e)).start()
        final[z, index] = mixed[k, z]

    project(0, x)
    remote(down_part(x_left, 1), down_part(x_left, 1), w_s.at[10], w_r.at[10], me).wait_recv()
    project(1, x_left)
    remote(down_part(x_right, 0), down_part(x_right, 0), w_s.at[11], w_r.at[11], me).wait_recv()
    project(2, x_right)
    remote(down_part(far, 0), down_part(far, 0), w_s.at[8], w_r.at[8], me).wait_recv()
    remote(down_part(far, 1), down_part(far, 1), w_s.at[9], w_r.at[9], me).wait_recv()
    project(3, far)
    gather(0, x)
    gather(1, x_left)
    gather(2, x_right)
    gather(3, far)
    for k in range(NX):
        for d in range(1, NZ):
            p = (z + d) % NZ
            remote(mixed.at[k, p], final.at[p, order[k]], fin_s.at[k, d], fin_r.at[k, p], me).wait_recv()
    pieces = [final[i // NX, i % NX].astype(F32) for i in range(n_ctx)]
    out_ref[0] = jnp.concatenate(pieces, axis=1).astype(BF16)

    lat_copy.wait_send()
    for d in range(1, NZ):
        remote(own_table, table.at[z], table_s.at[d], table_r.at[z], me).wait_send()
        remote(second, tokens.at[z], tok_s.at[d], tok_r.at[z], me).wait_send()
        for k in range(NX):
            remote(mixed.at[k, 0], final.at[z, 0], fin_s.at[k, d], fin_r.at[k, z], me).wait_send()
    for copy in (g_right, u_right, u_left, g_left, g_on, u_on, d_right, d_left, d_right_too, d_left_too, f_right, f_left, t_up, t_down):
        copy.wait_send()
    for d in (1, NZ - 1):
        remote(column, column, spread_s.at[d], spread_r.at[d], me).wait_send()
    for k in range(NX):
        for j, part_of in ((1, act_of(z, k)), (3, act_of(z, k)), (0, act_half(z_down, k, 0)), (2, act_half(z_up, k, 1))):
            remote(part_of, part_of, act_s.at[k, j], act_r.at[k, j], me).wait_send()
    others = pl.ds(0, n_exp - 1)
    remote(thin_send.at[others], thin_send.at[others], thin_s, thin_r, me).wait_send()
    remote(wide_send.at[others], wide_send.at[others], wide_s, wide_r, me).wait_send()
    for k in range(NX):
        remote(y_send.at[k, others], y_send.at[k, others], y_s.at[k], y_r.at[k], me).wait_send()


def settle_kernel(a_ref, b_ref, a_out, b_out):
    a_out[...] = a_ref[...]
    b_out[...] = b_ref[...]


def settle(a, b):
    whole = pl.BlockSpec(memory_space=pltpu.VMEM)
    return pl.pallas_call(
        settle_kernel,
        out_shape=(jax.ShapeDtypeStruct(a.shape, a.dtype), jax.ShapeDtypeStruct(b.shape, b.dtype)),
        in_specs=[whole, whole],
        out_specs=(whole, whole),
    )(a, b)


def on_device(hidden, queries, latents, expert_ids, route_weight, w_gate, w_up, w_down):
    n_exp = lax.axis_size("exp")
    tok, width = hidden.shape[1:]
    units, hid = w_gate.shape[1], w_down.shape[2]
    cols = w_down.shape[1]
    chunk = NZ * CAP
    slots = n_exp * chunk
    half = width // 2
    heads = queries.shape[1] // (LATENT + ROPE)
    dma = pltpu.SemaphoreType.DMA
    vmem = pl.BlockSpec(memory_space=pltpu.VMEM)
    hbm = pl.BlockSpec(memory_space=pltpu.HBM)
    moe_out, attended = pl.pallas_call(
        functools.partial(moe_kernel, n_exp),
        out_shape=(
            jax.ShapeDtypeStruct(hidden.shape, BF16),
            jax.ShapeDtypeStruct((queries.shape[0], heads * LATENT), BF16),
        ),
        in_specs=[vmem, vmem, vmem, vmem, vmem, hbm, hbm, hbm],
        out_specs=(vmem, vmem),
        scratch_shapes=[
            pltpu.VMEM(latents.shape[::-1], BF16),
            pltpu.VMEM((NZ, tok, width - half), BF16),
            pltpu.VMEM((NZ, 2 * tok, slots), F32),
            pltpu.VMEM((2 * tok, slots), F32),
            pltpu.VMEM((n_exp, chunk, half // NZ), BF16),
            pltpu.VMEM((n_exp, NZ, chunk, half // NZ), BF16),
            pltpu.VMEM((n_exp, chunk, width - half), BF16),
            pltpu.VMEM((n_exp, chunk, width - half), BF16),
            pltpu.VMEM((slots, width), BF16),
            pltpu.VMEM((NX * 2 * units, width), BF16),
            pltpu.VMEM((NX * cols, hid), BF16),
            pltpu.VMEM((NZ * NX * units, slots), BF16),
            pltpu.VMEM((NX, n_exp, chunk, cols), BF16),
            pltpu.VMEM((NX, n_exp, chunk, cols), BF16),
            pltpu.VMEM((NX, NZ, tok, cols), BF16),
            pltpu.VMEM((NZ, NX, tok, cols), BF16),
            dma((3,)),
            dma, dma,
            dma((NZ,)), dma((NZ,)), dma((NZ,)), dma((NZ,)),
            dma, dma,
            dma((NZ,)), dma((NZ,)),
            dma, dma,
            dma((12,)), dma((12,)),
            dma((NX, NZ)), dma((NX, NZ)),
            dma((NX,)), dma((NX,)),
            dma((NX, NZ)), dma((NX, NZ)),
        ],
        compiler_params=pltpu.CompilerParams(
            collective_id=0, has_side_effects=True, vmem_limit_bytes=56 << 20
        ),
    )(hidden, jnp.transpose(expert_ids, (2, 0, 1)), jnp.transpose(route_weight, (2, 0, 1)), queries, latents.T, w_gate, w_up, w_down)
    return settle(attended, moe_out)


def solution(mesh):
    placed = (
        P("exp", "ctx", None),
        P("ctx", "exp"),
        P("ctx", None),
        P("exp", "ctx", None),
        P("exp", "ctx", None),
        P("exp", "ctx", None),
        P("exp", "ctx", None),
        P("exp", "ctx", None),
    )
    return jax.shard_map(
        on_device,
        mesh=mesh,
        in_specs=placed,
        out_specs=(P("ctx", "exp"), P("exp", "ctx", None)),
        check_vma=False,
    )
```
